32 devices in a mesh: groups: 2 (over y), dp: 16 (over z, x, core).
Axes of the slice: x: 2, y: 2, z: 4, core: 2. Of those that a mesh axis runs over, the one named last changes fastest.
Arguments:
- merger_input: bfloat16 [3072, 2304], P(('groups', 'dp')), parts along dimension 0, may hold values from -6 to 6
- merger_weight: bfloat16 [2304, 2048], P('dp'), may hold values from -0.125 to 0.125
- merger_bias: float32 [2048], replicated, may hold values from -3 to 3
- norm_gain: float32 [2048], replicated, may hold values from 0.5 to 1.5
- gate_weight: bfloat16 [16, 2048, 768], P('dp'), may hold values from -0.125 to 0.125
- up_weight: bfloat16 [16, 2048, 768], P('dp'), may hold values from -0.125 to 0.125
- down_weight: bfloat16 [16, 768, 2048], P('dp'), may hold values from -0.21875 to 0.21875
- expert_ids: int32 [3072, 8], P(('groups', 'dp')), parts along dimension 0, may hold values from 0 to 15, all different within a row; in each aligned block of 96 rows (0 to 95, 96 to 191, ...) at most 72 rows name the same one
- combine_ints: int32 [3072, 8], P(('groups', 'dp')), parts along dimension 0, may hold values from 1 to 16
Outputs:
- mixed: bfloat16 [3072, 2048], P(('groups', 'dp')), parts along dimension 0
The draws below stay inside these ranges and needn't reach their ends.
There are 2 independent parts, one for each index of `groups`. The reference program is written for one: setup_inputs(seed, part) draws one part's arguments, and reference() takes and returns one part's arrays. A program takes and returns all parts, laid end to end along the dimension named above; an argument that names none is the same for every part. Nothing has to cross between parts.
Inputs may be any that keep to these rules, and one draw needn't show every extreme that they name: `expert_ids`: each row names 8 different experts; in the rows of one device no expert is named more than 72 times, and that many is reached.
All inputs are finite; a program needn't handle non-finite values.
Results may differ from the reference program's by a relative error of at most 0.0051.
Values may be sent and summed in bfloat16 or wider, within the bound.
No kernel may reach another device: no remote copies, remote signals or barrier semaphores. Data moves between devices by JAX's collectives and lax.ppermute only.
A program may use at most 128 MiB of HBM per device.

```python
import math
import jax
import jax.numpy as jnp
import numpy as np
from jax import lax

D = 2048
EXPERT_HIDDEN = 768
MERGE = 2304
TOP = 8
ROWS_DEV = 96
EXPERTS = 16
ROWS = 1536
CAP = 72
N_DP = 16


def plant(drawn, own_key, low, largest):
    longest = drawn.shape.index(max(drawn.shape))
    spots = []
    for shift in (0, 1):
        where = [jax.random.randint(jax.random.fold_in(own_key, axis), (), 0, length) for axis, length in enumerate(drawn.shape)]
        where[longest] = (where[longest] + shift) % drawn.shape[longest]
        spots.append(tuple(where))
    return drawn.at[spots[0]].set(low).at[spots[1]].set(largest)


def block_scale(own_key, extent, shards, least, top_value):
    def one(dim, blocks):
        steps = jax.random.uniform(jax.random.fold_in(jax.random.fold_in(own_key, 6), dim), (blocks,), jnp.float32, least / len(shards), top_value / len(shards))
        return jnp.repeat(jnp.exp(steps), extent[dim] // blocks).reshape((-1,) + (1,) * (len(extent) - dim - 1))

    gain = one(*shards[0])
    for cut in shards[1:]:
        gain = gain * one(*cut)
    return gain


def deal_out(rng, own, number, rows, amount, top, most, lean):
    ranking = jax.random.permutation(rng, amount)
    heavy_load, usual = shares(amount, rows * top, most, lean, True), shares(amount, rows * top, most, lean, False)
    places = jnp.arange(amount)

    def named(sizes, offset_by):
        used = int((sizes > 0).sum())
        fixed = max(1, used // 4)
        moved = fixed + (places - fixed + offset_by * (used - fixed)) % max(1, amount - fixed)
        return jnp.zeros((amount,), jnp.int32).at[ranking[jnp.where(places < fixed, places, moved)]].set(jnp.asarray(sizes, jnp.int32))

    sizes = jnp.where(number % 4 == 0, named(heavy_load, number // 4), named(usual, number - number // 4 - 1))
    mixed = jax.random.permutation(jax.random.fold_in(own, 3), amount)
    giver, sink = mixed[0:amount // 2 * 2:2], mixed[1:amount // 2 * 2:2]
    slack = jnp.minimum(sizes[giver] - 1, most - sizes[sink]) // 2
    slack = jnp.where((giver == ranking[0]) | (sink == ranking[0]) | (sizes[sink] == 0), 0, jnp.maximum(slack, 0))
    moved = jax.random.randint(jax.random.fold_in(own, 4), (amount // 2,), 0, 1 << 20) % (slack + 1)
    sizes = sizes.at[giver].add(-moved).at[sink].add(moved)
    items = jnp.searchsorted(jnp.cumsum(sizes), jnp.arange(rows * top), side="right").astype(jnp.int32)
    table = items.reshape(top, rows).T
    table = table[jax.random.permutation(jax.random.fold_in(own, 1), rows)]
    offset_by = jax.random.randint(jax.random.fold_in(own, 2), (rows, 1), 0, top)
    return jnp.take_along_axis(table, (jnp.arange(top)[None, :] + offset_by) % top, axis=1)


def shares(number_of, total, reach, lean, full):
    loads = [(1 << 20) // math.isqrt(standing ** lean) + 1 for standing in range(1, number_of + 1)]
    largest = reach if full else min(reach, max(-(-total // number_of), total * loads[0] // sum(loads)))
    least = 1 if total - largest >= number_of - 1 else 0
    given, rest = [largest] + [least] * (number_of - 1), total - largest - least * (number_of - 1)
    while rest > 0:
        candidates = [i for i in range(1, number_of) if given[i] < largest] or [i for i in range(1, number_of) if given[i] < reach]
        whole, remaining = sum([loads[i] for i in candidates]), rest
        for i in candidates:
            addition = min(reach - given[i], max(1, remaining * loads[i] // whole), rest)
            given[i] = given[i] + addition
            rest = rest - addition
    return np.array(given)


def normal_values(rng, dims, deviation, reach, shards=(), kind=jnp.bfloat16):
    array = deviation * jax.random.normal(rng, dims, jnp.float32)
    if shards:
        array = array * block_scale(rng, dims, shards, -0.22, 0.18)
    return jnp.clip(array, -reach, reach).astype(kind)


def setup_inputs(seed: int = 0, part: int = 0) -> dict:
    arg_keys = jax.random.split(jax.random.key(seed), 10)
    part_keys = jax.random.split(jax.random.fold_in(arg_keys[9], part), 10)
    merger_input = normal_values(part_keys[0], (ROWS, MERGE), 1.0, 6.0, ((0, 16),))
    merger_weight = normal_values(arg_keys[1], (MERGE, D), MERGE ** -0.5, 0.125, ((0, 16),))
    merger_bias = normal_values(arg_keys[2], (D,), 0.5, 3.0, (), jnp.float32)
    norm_gain = jnp.clip(jax.random.uniform(arg_keys[3], (D,), jnp.float32, 0.5, 1.5), 0.5, 1.5)
    gate_weight = normal_values(arg_keys[4], (EXPERTS, D, EXPERT_HIDDEN), D ** -0.5, 0.125, ((0, 16),))
    up_weight = normal_values(arg_keys[5], (EXPERTS, D, EXPERT_HIDDEN), D ** -0.5, 0.125, ((0, 16),))
    down_weight = normal_values(arg_keys[6], (EXPERTS, EXPERT_HIDDEN, D), EXPERT_HIDDEN ** -0.5, 0.21875, ((0, 16),))
    expert_ids_keys = jax.random.split(jax.random.fold_in(part_keys[7], 1), ROWS // ROWS_DEV)
    expert_ids_turns = jax.random.permutation(jax.random.fold_in(part_keys[7], 3), ROWS // ROWS_DEV)
    expert_ids = jax.vmap(lambda own, number: deal_out(jax.random.fold_in(part_keys[7], 2), own, number, ROWS_DEV, EXPERTS, TOP, CAP, 2))(expert_ids_keys, expert_ids_turns).reshape((ROWS, TOP))
    combine_ints = plant(jax.random.randint(part_keys[8], (ROWS, TOP), 1, 17), jax.random.fold_in(part_keys[8], 1), 1, 16).astype(jnp.int32)
    return dict(merger_input=merger_input, merger_weight=merger_weight, merger_bias=merger_bias, norm_gain=norm_gain, gate_weight=gate_weight, up_weight=up_weight, down_weight=down_weight, expert_ids=expert_ids, combine_ints=combine_ints)


def reference(merger_input, merger_weight, merger_bias, norm_gain, gate_weight, up_weight, down_weight, expert_ids, combine_ints):
    act = jax.nn.gelu(merger_input.astype(jnp.float32), approximate=False).astype(jnp.bfloat16)
    merged = jnp.dot(act, merger_weight, preferred_element_type=jnp.float32) + merger_bias
    scale = lax.rsqrt(lax.optimization_barrier(jnp.mean(merged * merged, axis=1, keepdims=True)) + 1e-06)
    normed = (merged * scale * norm_gain).astype(jnp.bfloat16)
    onehot = (expert_ids[:, :, None] == jnp.arange(EXPERTS, dtype=jnp.int32)[None, None, :]).astype(jnp.int32)
    blocks = onehot.reshape(N_DP, ROWS_DEV * TOP, EXPERTS)
    before = jnp.cumsum(blocks, axis=1) - blocks
    position = lax.optimization_barrier(jnp.sum(before * blocks, axis=2)).reshape(ROWS, TOP)
    block_id = (jnp.arange(ROWS, dtype=jnp.int32) // ROWS_DEV)[:, None]
    slot = (block_id * CAP + position).astype(jnp.int32)
    row_index = jnp.broadcast_to(jnp.arange(ROWS, dtype=jnp.int32)[:, None], (ROWS, TOP))
    table = jnp.full((EXPERTS, N_DP * CAP), ROWS, jnp.int32).at[expert_ids, slot].set(row_index)
    padded = jnp.concatenate([normed, jnp.zeros((1, D), jnp.bfloat16)], axis=0)

    def serve(expert):
        inputs = padded[table[expert]].astype(jnp.float32)
        gate = jnp.dot(inputs, gate_weight[expert].astype(jnp.float32))
        up = jnp.dot(inputs, up_weight[expert].astype(jnp.float32))
        hidden = (jax.nn.silu(gate) * up).astype(jnp.bfloat16)
        return jnp.dot(hidden.astype(jnp.float32), down_weight[expert].astype(jnp.float32)).astype(jnp.bfloat16)
    results = lax.map(serve, jnp.arange(EXPERTS, dtype=jnp.int32))
    picked = results[expert_ids, slot]
    counts = combine_ints.astype(jnp.float32)
    weights = counts / lax.optimization_barrier(jnp.sum(counts, axis=1, keepdims=True))
    combined = lax.optimization_barrier(jnp.sum(weights[:, :, None] * picked.astype(jnp.float32), axis=1))
    return (merged + combined).astype(jnp.bfloat16)
```

```python
import functools

import jax
import jax.numpy as jnp
from jax import lax
from jax.sharding import PartitionSpec as P


def run_experts(received, gate_weight, up_weight, down_weight, ndevices):
    local = gate_weight.shape[0]
    slots = received.shape[1]
    width = received.shape[2]
    inputs = received.reshape(ndevices, local, slots, width)
    gate = jnp.einsum("jlcd,ldh->jlch", inputs, gate_weight, preferred_element_type=jnp.float32)
    up = jnp.einsum("jlcd,ldh->jlch", inputs, up_weight, preferred_element_type=jnp.float32)
    hidden = (jax.nn.silu(gate) * up).astype(jnp.bfloat16)
    output = jnp.einsum("jlch,lhd->jlcd", hidden, down_weight, preferred_element_type=jnp.float32)
    return output.astype(jnp.bfloat16).reshape(ndevices * local, slots, width)


def routed(
    merger_input,
    merger_weight,
    merger_bias,
    norm_gain,
    gate_weight,
    up_weight,
    down_weight,
    expert_ids,
    combine_ints,
):
    ndevices = lax.axis_size("dp")
    rows = merger_input.shape[0]
    width = merger_weight.shape[1]
    choose = expert_ids.shape[1]
    experts_all = gate_weight.shape[0] * ndevices
    capacity = (3 * rows * choose + 2 * ndevices - 1) // (2 * ndevices)
    act = jax.nn.gelu(merger_input.astype(jnp.float32), approximate=False).astype(jnp.bfloat16)
    merged = jnp.dot(
        act,
        lax.all_gather(merger_weight, "dp", axis=0, tiled=True),
        preferred_element_type=jnp.float32,
    )
    merged = merged + merger_bias
    scale = lax.rsqrt(jnp.mean(merged * merged, axis=1, keepdims=True) + 1e-06)
    normed = (merged * scale * norm_gain).astype(jnp.bfloat16)
    onehot = (
        expert_ids[:, :, None] == jnp.arange(experts_all, dtype=jnp.int32)[None, None, :]
    ).astype(jnp.int32)
    flat_hot = onehot.reshape(rows * choose, experts_all)
    before = jnp.cumsum(flat_hot, axis=0) - flat_hot
    position = jnp.sum(before * flat_hot, axis=1)
    slot_flat = expert_ids.reshape(rows * choose) * capacity + position
    repeated = jnp.repeat(normed, choose, axis=0)
    outgoing = jnp.zeros((experts_all * capacity, width), jnp.bfloat16).at[slot_flat].set(repeated)
    outgoing = outgoing.reshape(experts_all, capacity, width)
    received = lax.all_to_all(outgoing, "dp", split_axis=0, concat_axis=0, tiled=True)
    served = run_experts(received, gate_weight, up_weight, down_weight, ndevices)
    returned = lax.all_to_all(served, "dp", split_axis=0, concat_axis=0, tiled=True)
    returned = returned.reshape(experts_all * capacity, width)
    picked = returned[slot_flat].reshape(rows, choose, width)
    counts = combine_ints.astype(jnp.float32)
    weights = counts / jnp.sum(counts, axis=1, keepdims=True)
    combined = jnp.sum(weights[:, :, None] * picked.astype(jnp.float32), axis=1)
    return (merged + combined).astype(jnp.bfloat16)


def swap_pairs(n):
    return [(i, i ^ 1) for i in range(n)]


def ring_order(chips):
    half = chips // 2
    return [2 * z for z in range(half)] + [2 * z + 1 for z in reversed(range(half))]


def ring_pairs(chips, by):
    order = ring_order(chips)
    pairs = []
    for spot, chip in enumerate(order):
        target = order[(spot + by) % chips]
        pairs += [(2 * chip, 2 * target), (2 * chip + 1, 2 * target + 1)]
    return pairs


def serve(block, share, experts):
    total = None
    for (gate_weight, up_weight, down_weight), weight in zip(experts, share):
        gate = jnp.dot(block, gate_weight, preferred_element_type=jnp.float32)
        up = jnp.dot(block, up_weight, preferred_element_type=jnp.float32)
        hidden = (jax.nn.silu(gate) * up * weight[:, None]).astype(jnp.bfloat16)
        part = jnp.dot(hidden, down_weight, preferred_element_type=jnp.float32)
        total = part if total is None else total + part
    return total


def dense(
    merger_input,
    merger_weight,
    merger_bias,
    norm_gain,
    gate_weight,
    up_weight,
    down_weight,
    expert_ids,
    combine_ints,
):
    n = lax.axis_size("dp")
    chips = n // 2
    far = chips // 2
    rows = merger_input.shape[0]
    depth, width = merger_weight.shape
    order = ring_order(chips)
    ring = jnp.asarray(order + order + order, jnp.int32)
    spot_of = jnp.asarray([order.index(chip) for chip in range(chips)], jnp.int32)
    me = lax.axis_index("dp")
    core = me % 2
    spot = spot_of[me // 2] + chips

    swap = functools.partial(lax.ppermute, axis_name="dp", perm=swap_pairs(n))
    ahead = functools.partial(lax.ppermute, axis_name="dp", perm=ring_pairs(chips, 1))
    back = functools.partial(lax.ppermute, axis_name="dp", perm=ring_pairs(chips, -1))

    counts = combine_ints.astype(jnp.float32)
    weights = counts / jnp.sum(counts, axis=1, keepdims=True)
    named = expert_ids[:, :, None] == jnp.arange(n, dtype=jnp.int32)[None, None, :]
    spread = jnp.sum(jnp.where(named, weights[:, :, None], 0.0), axis=1)
    spread = spread.T.reshape(chips, 2, rows)
    planes = [[2 * chip + side for chip in range(chips)] for side in range(2)]
    shares = lax.all_to_all(
        spread, "dp", split_axis=0, concat_axis=0, tiled=True, axis_index_groups=planes
    )
    shares = jnp.where(core == 0, shares, shares[:, ::-1])

    mine = (gate_weight[0], up_weight[0], down_weight[0])
    experts = (mine, tuple(swap(w) for w in mine))

    act = jax.nn.gelu(merger_input.astype(jnp.float32), approximate=False).astype(jnp.bfloat16)
    act = act.reshape(rows, chips, 2, depth).transpose(2, 1, 0, 3)
    kept = lax.dynamic_index_in_dim(act, core, 0, keepdims=False)
    given = lax.dynamic_index_in_dim(act, 1 - core, 0, keepdims=False)
    both = jnp.concatenate([kept, swap(given)], axis=1)

    def term(offset, weight, low, high):
        block = lax.dynamic_index_in_dim(both, ring[spot + offset], 0, keepdims=False)
        return jnp.dot(block[:, low:high], weight, preferred_element_type=jnp.float32)

    left = right = merger_weight
    total = term(0, merger_weight, 0, depth)
    for step in range(1, far):
        left, right = ahead(left), back(right)
        total = total + term(-step, left, 0, depth) + term(step, right, 0, depth)
    mid = depth // 2
    total = total + term(-far, ahead(left[:mid]), 0, mid) + term(far, back(right[mid:]), mid, depth)
    merged = total[:rows] + swap(total[rows:]) + merger_bias
    scale = lax.rsqrt(jnp.mean(merged * merged, axis=1, keepdims=True) + 1e-06)
    normed = (merged * scale * norm_gain).astype(jnp.bfloat16)

    def share_of(offset):
        return lax.dynamic_index_in_dim(shares, ring[spot + offset], 0, keepdims=False)

    lefts, rights = [normed], [normed]
    for step in range(1, far):
        lefts.append(ahead(lefts[-1]))
        rights.append(back(rights[-1]))
    cut = rows // 2
    last = [ahead(lefts[-1][:cut]), back(rights[-1][cut:])]
    own = serve(normed, share_of(0), experts)
    pairs = []
    for step in range(1, far):
        block = jnp.concatenate([lefts[step], rights[step]], axis=0)
        share = jnp.concatenate([share_of(-step), share_of(step)], axis=1)
        pairs.append(serve(block, share, experts))
    farthest = serve(jnp.concatenate(last, axis=0), share_of(far), experts)

    top, bottom = ahead(farthest[:cut].astype(jnp.bfloat16)), back(farthest[cut:].astype(jnp.bfloat16))
    for step in reversed(range(1, far)):
        block = pairs[step - 1]
        to_ahead, to_back = block[rows:], block[:rows]
        if step == far - 1:
            top = jnp.pad(top.astype(jnp.float32), ((0, rows - cut), (0, 0)))
            bottom = jnp.pad(bottom.astype(jnp.float32), ((cut, 0), (0, 0)))
        top = ahead((to_ahead + top.astype(jnp.float32)).astype(jnp.bfloat16))
        bottom = back((to_back + bottom.astype(jnp.float32)).astype(jnp.bfloat16))
    combined = own + top.astype(jnp.float32) + bottom.astype(jnp.float32)
    return (merged + combined).astype(jnp.bfloat16)


def shards(*arrays):
    merger_input, gate_weight, expert_ids = arrays[0], arrays[4], arrays[7]
    n = lax.axis_size("dp")
    rows, choose = expert_ids.shape
    capacity = (3 * rows * choose + 2 * n - 1) // (2 * n)
    if gate_weight.shape[0] == 1 and n % 4 == 0 and n >= 8 and 2 * capacity >= rows:
        return dense(*arrays)
    return routed(*arrays)


def solution(mesh):
    placed = (
        P(("groups", "dp"), None),
        P("dp", None),
        P(),
        P(),
        P("dp", None, None),
        P("dp", None, None),
        P("dp", None, None),
        P(("groups", "dp"), None),
        P(("groups", "dp"), None),
    )
    return jax.shard_map(
        shards, mesh=mesh, in_specs=placed, out_specs=P(("groups", "dp"), None), check_vma=False
    )
```

```python
import functools

import jax
import jax.numpy as jnp
from jax import lax
from jax.experimental import pallas as pl
from jax.experimental.pallas import tpu as pltpu
from jax.sharding import PartitionSpec as P


def run_experts(received, gate_weight, up_weight, down_weight, ndevices):
    local = gate_weight.shape[0]
    slots = received.shape[1]
    width = received.shape[2]
    inputs = received.reshape(ndevices, local, slots, width)
    gate = jnp.einsum("jlcd,ldh->jlch", inputs, gate_weight, preferred_element_type=jnp.float32)
    up = jnp.einsum("jlcd,ldh->jlch", inputs, up_weight, preferred_element_type=jnp.float32)
    hidden = (jax.nn.silu(gate) * up).astype(jnp.bfloat16)
    output = jnp.einsum("jlch,lhd->jlcd", hidden, down_weight, preferred_element_type=jnp.float32)
    return output.astype(jnp.bfloat16).reshape(ndevices * local, slots, width)


def routed(
    merger_input,
    merger_weight,
    merger_bias,
    norm_gain,
    gate_weight,
    up_weight,
    down_weight,
    expert_ids,
    combine_ints,
):
    ndevices = lax.axis_size("dp")
    rows = merger_input.shape[0]
    width = merger_weight.shape[1]
    choose = expert_ids.shape[1]
    experts_all = gate_weight.shape[0] * ndevices
    capacity = (3 * rows * choose + 2 * ndevices - 1) // (2 * ndevices)
    act = jax.nn.gelu(merger_input.astype(jnp.float32), approximate=False).astype(jnp.bfloat16)
    merged = jnp.dot(
        act,
        lax.all_gather(merger_weight, "dp", axis=0, tiled=True),
        preferred_element_type=jnp.float32,
    )
    merged = merged + merger_bias
    scale = lax.rsqrt(jnp.mean(merged * merged, axis=1, keepdims=True) + 1e-06)
    normed = (merged * scale * norm_gain).astype(jnp.bfloat16)
    onehot = (
        expert_ids[:, :, None] == jnp.arange(experts_all, dtype=jnp.int32)[None, None, :]
    ).astype(jnp.int32)
    flat_hot = onehot.reshape(rows * choose, experts_all)
    before = jnp.cumsum(flat_hot, axis=0) - flat_hot
    position = jnp.sum(before * flat_hot, axis=1)
    slot_flat = expert_ids.reshape(rows * choose) * capacity + position
    repeated = jnp.repeat(normed, choose, axis=0)
    outgoing = jnp.zeros((experts_all * capacity, width), jnp.bfloat16).at[slot_flat].set(repeated)
    outgoing = outgoing.reshape(experts_all, capacity, width)
    received = lax.all_to_all(outgoing, "dp", split_axis=0, concat_axis=0, tiled=True)
    served = run_experts(received, gate_weight, up_weight, down_weight, ndevices)
    returned = lax.all_to_all(served, "dp", split_axis=0, concat_axis=0, tiled=True)
    returned = returned.reshape(experts_all * capacity, width)
    picked = returned[slot_flat].reshape(rows, choose, width)
    counts = combine_ints.astype(jnp.float32)
    weights = counts / jnp.sum(counts, axis=1, keepdims=True)
    combined = jnp.sum(weights[:, :, None] * picked.astype(jnp.float32), axis=1)
    return (merged + combined).astype(jnp.bfloat16)


LANES = 128


def swap_pairs(n):
    return [(i, i ^ 1) for i in range(n)]


def ring_order(chips):
    half = chips // 2
    return [2 * z for z in range(half)] + [2 * z + 1 for z in reversed(range(half))]


def ring_pairs(chips, by):
    order = ring_order(chips)
    pairs = []
    for spot, chip in enumerate(order):
        target = order[(spot + by) % chips]
        pairs += [(2 * chip, 2 * target), (2 * chip + 1, 2 * target + 1)]
    return pairs


def tile_of(extent, most):
    return max(t for t in range(LANES, most + 1, LANES) if extent % t == 0)


def serve_body(columns, blocks, *refs):
    ins, share_ref = refs[:blocks], refs[blocks]
    gate_ref, up_ref, down_ref, own_ref, other_ref, x_ref, h_ref = refs[blocks + 1 :]
    width, wide = gate_ref.shape
    start = 0
    share = []
    for ref, (column, low, high) in zip(ins, columns):
        size = ref.shape[0]
        x_ref[start : start + size, :] = ref[...]
        share.append(share_ref[low:high, column : column + 1])
        start += size
    share = jnp.concatenate(share, axis=0)
    tile = tile_of(wide, 256)
    for at in range(0, wide, tile):
        x = x_ref[...]
        gate = jnp.dot(x, gate_ref[:, at : at + tile], preferred_element_type=jnp.float32)
        up = jnp.dot(x, up_ref[:, at : at + tile], preferred_element_type=jnp.float32)
        h_ref[:, at : at + tile] = (gate * (1.0 / (1.0 + jnp.exp(-gate))) * up * share).astype(jnp.bfloat16)
    half = start // 2
    tile = tile_of(width, 512)
    for at in range(0, width, tile):
        out = jnp.dot(h_ref[...], down_ref[:, at : at + tile], preferred_element_type=jnp.float32)
        own_ref[:, at : at + tile] = out[:half].astype(jnp.bfloat16)
        other_ref[:, at : at + tile] = out[half:].astype(jnp.bfloat16)


def serve(ins, columns, share, experts):
    rows = sum(x.shape[0] for x in ins)
    width, wide = experts[0].shape
    vmem = pl.BlockSpec(memory_space=pltpu.VMEM)
    return pl.pallas_call(
        functools.partial(serve_body, columns, len(ins)),
        out_shape=[jax.ShapeDtypeStruct((rows // 2, width), jnp.bfloat16)] * 2,
        in_specs=[vmem] * (len(ins) + 4),
        out_specs=[vmem, vmem],
        scratch_shapes=[pltpu.VMEM((rows, width), jnp.bfloat16), pltpu.VMEM((rows, wide), jnp.bfloat16)],
        compiler_params=pltpu.CompilerParams(vmem_limit_bytes=VMEM_LIMIT),
        cost_estimate=pl.CostEstimate(
            flops=6 * rows * width * wide, bytes_accessed=6 * width * wide, transcendentals=rows * wide
        ),
        name="serve",
    )(*ins, share, *experts)


VMEM_LIMIT = 24 * 1024 * 1024


def around(array, order, spot):
    ring = jnp.stack([array[chip] for chip in order] * 2)
    zero = jnp.uint32(0)
    return lax.dynamic_slice(ring, (spot,) + (zero,) * (array.ndim - 1), array.shape)


def dense(
    merger_input,
    merger_weight,
    merger_bias,
    norm_gain,
    gate_weight,
    up_weight,
    down_weight,
    expert_ids,
    combine_ints,
):
    n = lax.axis_size("dp")
    chips = n // 2
    far = chips // 2
    rows = merger_input.shape[0]
    depth, _ = merger_weight.shape
    order = ring_order(chips)
    me = lax.axis_index("dp").astype(jnp.uint32)
    core = me & 1
    spot = jnp.where((me & 2) == 0, me >> 2, jnp.uint32(chips - 1) - (me >> 2))

    swap = functools.partial(lax.ppermute, axis_name="dp", perm=swap_pairs(n))
    ahead = functools.partial(lax.ppermute, axis_name="dp", perm=ring_pairs(chips, 1))
    back = functools.partial(lax.ppermute, axis_name="dp", perm=ring_pairs(chips, -1))

    counts = combine_ints.astype(jnp.float32)
    weights = counts / jnp.sum(counts, axis=1, keepdims=True)
    named = expert_ids[:, :, None] == jnp.arange(n, dtype=jnp.int32)[None, None, :]
    spread = jnp.sum(jnp.where(named, weights[:, :, None], 0.0), axis=1)
    share = lax.all_to_all(spread.T, "dp", split_axis=0, concat_axis=0, tiled=True)
    share = share.reshape(chips, 2, rows)
    share = jnp.where(core == 0, share, share[:, ::-1])
    share = around(share, order, spot).reshape(n, rows).T

    act = jax.nn.gelu(merger_input.astype(jnp.float32), approximate=False).astype(jnp.bfloat16)
    act = act.reshape(rows, chips, 2, depth)
    first, second = act[:, :, 0], act[:, :, 1]
    kept = jnp.where(core == 0, first, second)
    given = jnp.where(core == 0, second, first)
    both = jnp.concatenate([kept, swap(given)], axis=0).transpose(1, 0, 2)
    both = around(both, order, spot)

    def term(offset, weight, low, high):
        block = both[offset % chips]
        return jnp.dot(block[:, low:high], weight, preferred_element_type=jnp.float32)

    left = right = merger_weight
    total = term(0, merger_weight, 0, depth)
    for step in range(1, far):
        left, right = ahead(left), back(right)
        total = total + term(-step, left, 0, depth) + term(step, right, 0, depth)
    mid = depth // 2
    total = total + term(far, ahead(left[:mid]), 0, mid) + term(far, back(right[mid:]), mid, depth)
    merged = total[:rows] + swap(total[rows:]) + merger_bias
    scale = lax.rsqrt(jnp.mean(merged * merged, axis=1, keepdims=True) + 1e-06)
    normed = (merged * scale * norm_gain).astype(jnp.bfloat16)

    experts = [w[0] for w in (gate_weight, up_weight, down_weight)]
    cut = rows // 2
    left = right = normed
    other = swap(normed)
    outs = [serve([normed, other], [(0, 0, rows), (1, 0, rows)], share, experts)]
    for step in range(1, far + 1):
        if step < far:
            lo, hi = 2 * (chips - step), 2 * step
            columns = [(lo, 0, rows), (hi, 0, rows), (lo + 1, 0, rows), (hi + 1, 0, rows)]
        else:
            left, right = left[:cut], right[cut:]
            lo = 2 * far
            columns = [(lo, 0, cut), (lo, cut, rows), (lo + 1, 0, cut), (lo + 1, cut, rows)]
        left = ahead(left)
        right = back(right)
        left_other, right_other = swap(left), swap(right)
        outs.append(serve([left, right, left_other, right_other], columns, share, experts))
    sums = [own.astype(jnp.float32) + swap(other).astype(jnp.float32) for own, other in outs]
    top, bottom = ahead(sums[far][:cut].astype(jnp.bfloat16)), back(sums[far][cut:].astype(jnp.bfloat16))
    top = jnp.pad(top, ((0, rows - cut), (0, 0)))
    bottom = jnp.pad(bottom, ((cut, 0), (0, 0)))
    for step in reversed(range(1, far)):
        to_back, to_ahead = sums[step][:rows], sums[step][rows:]
        top = ahead((to_ahead + top.astype(jnp.float32)).astype(jnp.bfloat16))
        bottom = back((to_back + bottom.astype(jnp.float32)).astype(jnp.bfloat16))
    combined = sums[0] + top.astype(jnp.float32) + bottom.astype(jnp.float32)
    return (merged + combined).astype(jnp.bfloat16)


def shards(*arrays):
    gate_weight, expert_ids = arrays[4], arrays[7]
    n = lax.axis_size("dp")
    rows, choose = expert_ids.shape
    capacity = (3 * rows * choose + 2 * n - 1) // (2 * n)
    if gate_weight.shape[0] == 1 and n % 4 == 0 and n >= 8 and 2 * capacity >= rows:
        return dense(*arrays)
    return routed(*arrays)


def solution(mesh):
    placed = (
        P(("groups", "dp"), None),
        P("dp", None),
        P(),
        P(),
        P("dp", None, None),
        P("dp", None, None),
        P("dp", None, None),
        P(("groups", "dp"), None),
        P(("groups", "dp"), None),
    )
    return jax.shard_map(
        shards, mesh=mesh, in_specs=placed, out_specs=P(("groups", "dp"), None), check_vma=False
    )
```

```python
import functools

import jax
import jax.numpy as jnp
from jax import lax
from jax.experimental import pallas as pl
from jax.experimental.pallas import tpu as pltpu
from jax.sharding import PartitionSpec as P


def run_experts(received, gate_weight, up_weight, down_weight, ndevices):
    local = gate_weight.shape[0]
    slots = received.shape[1]
    width = received.shape[2]
    inputs = received.reshape(ndevices, local, slots, width)
    gate = jnp.einsum("jlcd,ldh->jlch", inputs, gate_weight, preferred_element_type=jnp.float32)
    up = jnp.einsum("jlcd,ldh->jlch", inputs, up_weight, preferred_element_type=jnp.float32)
    hidden = (jax.nn.silu(gate) * up).astype(jnp.bfloat16)
    output = jnp.einsum("jlch,lhd->jlcd", hidden, down_weight, preferred_element_type=jnp.float32)
    return output.astype(jnp.bfloat16).reshape(ndevices * local, slots, width)


def routed(
    merger_input,
    merger_weight,
    merger_bias,
    norm_gain,
    gate_weight,
    up_weight,
    down_weight,
    expert_ids,
    combine_ints,
):
    ndevices = lax.axis_size("dp")
    rows = merger_input.shape[0]
    width = merger_weight.shape[1]
    choose = expert_ids.shape[1]
    experts_all = gate_weight.shape[0] * ndevices
    capacity = (3 * rows * choose + 2 * ndevices - 1) // (2 * ndevices)
    act = jax.nn.gelu(merger_input.astype(jnp.float32), approximate=False).astype(jnp.bfloat16)
    merged = jnp.dot(
        act,
        lax.all_gather(merger_weight, "dp", axis=0, tiled=True),
        preferred_element_type=jnp.float32,
    )
    merged = merged + merger_bias
    scale = lax.rsqrt(jnp.mean(merged * merged, axis=1, keepdims=True) + 1e-06)
    normed = (merged * scale * norm_gain).astype(jnp.bfloat16)
    onehot = (
        expert_ids[:, :, None] == jnp.arange(experts_all, dtype=jnp.int32)[None, None, :]
    ).astype(jnp.int32)
    flat_hot = onehot.reshape(rows * choose, experts_all)
    before = jnp.cumsum(flat_hot, axis=0) - flat_hot
    position = jnp.sum(before * flat_hot, axis=1)
    slot_flat = expert_ids.reshape(rows * choose) * capacity + position
    repeated = jnp.repeat(normed, choose, axis=0)
    outgoing = jnp.zeros((experts_all * capacity, width), jnp.bfloat16).at[slot_flat].set(repeated)
    outgoing = outgoing.reshape(experts_all, capacity, width)
    received = lax.all_to_all(outgoing, "dp", split_axis=0, concat_axis=0, tiled=True)
    served = run_experts(received, gate_weight, up_weight, down_weight, ndevices)
    returned = lax.all_to_all(served, "dp", split_axis=0, concat_axis=0, tiled=True)
    returned = returned.reshape(experts_all * capacity, width)
    picked = returned[slot_flat].reshape(rows, choose, width)
    counts = combine_ints.astype(jnp.float32)
    weights = counts / jnp.sum(counts, axis=1, keepdims=True)
    combined = jnp.sum(weights[:, :, None] * picked.astype(jnp.float32), axis=1)
    return (merged + combined).astype(jnp.bfloat16)


LANES = 128


def swap_pairs(n):
    return [(i, i ^ 1) for i in range(n)]


def ring_order(chips):
    half = chips // 2
    return [2 * z for z in range(half)] + [2 * z + 1 for z in reversed(range(half))]


def ring_pairs(chips, by):
    order = ring_order(chips)
    pairs = []
    for spot, chip in enumerate(order):
        target = order[(spot + by) % chips]
        pairs += [(2 * chip, 2 * target), (2 * chip + 1, 2 * target + 1)]
    return pairs


def tile_of(extent, most):
    return max(t for t in range(LANES, most + 1, LANES) if extent % t == 0)


def serve_body(columns, blocks, *refs):
    ins, share_ref = refs[:blocks], refs[blocks]
    gate_ref, up_ref, down_ref, own_ref, other_ref, x_ref, h_ref = refs[blocks + 1 :]
    width, wide = gate_ref.shape
    start = 0
    share = []
    for ref, (column, low, high) in zip(ins, columns):
        size = ref.shape[0]
        x_ref[start : start + size, :] = ref[...]
        share.append(share_ref[low:high, column : column + 1])
        start += size
    share = jnp.concatenate(share, axis=0)
    tile = tile_of(wide, 256)
    for at in range(0, wide, tile):
        x = x_ref[...]
        gate = jnp.dot(x, gate_ref[:, at : at + tile], preferred_element_type=jnp.float32)
        up = jnp.dot(x, up_ref[:, at : at + tile], preferred_element_type=jnp.float32)
        h_ref[:, at : at + tile] = (gate * (1.0 / (1.0 + jnp.exp(-gate))) * up * share).astype(jnp.bfloat16)
    half = start // 2
    tile = tile_of(width, 512)
    for at in range(0, width, tile):
        out = jnp.dot(h_ref[...], down_ref[:, at : at + tile], preferred_element_type=jnp.float32)
        own_ref[:, at : at + tile] = out[:half].astype(jnp.bfloat16)
        other_ref[:, at : at + tile] = out[half:].astype(jnp.bfloat16)


def serve(ins, columns, share, experts):
    rows = sum(x.shape[0] for x in ins)
    width, wide = experts[0].shape
    vmem = pl.BlockSpec(memory_space=pltpu.VMEM)
    return pl.pallas_call(
        functools.partial(serve_body, columns, len(ins)),
        out_shape=[jax.ShapeDtypeStruct((rows // 2, width), jnp.bfloat16)] * 2,
        in_specs=[vmem] * (len(ins) + 4),
        out_specs=[vmem, vmem],
        scratch_shapes=[pltpu.VMEM((rows, width), jnp.bfloat16), pltpu.VMEM((rows, wide), jnp.bfloat16)],
        compiler_params=pltpu.CompilerParams(vmem_limit_bytes=VMEM_LIMIT),
        cost_estimate=pl.CostEstimate(
            flops=6 * rows * width * wide, bytes_accessed=6 * width * wide, transcendentals=rows * wide
        ),
        name="serve",
    )(*ins, share, *experts)


VMEM_LIMIT = 24 * 1024 * 1024


def around(array, spot):
    ring = [array[0::2], array[1::2][::-1]] * 2
    zero = jnp.uint32(0)
    return lax.dynamic_slice(jnp.concatenate(ring), (spot,) + (zero,) * (array.ndim - 1), array.shape)


def dense(
    merger_input,
    merger_weight,
    merger_bias,
    norm_gain,
    gate_weight,
    up_weight,
    down_weight,
    expert_ids,
    combine_ints,
):
    n = lax.axis_size("dp")
    chips = n // 2
    far = chips // 2
    rows = merger_input.shape[0]
    depth, width = merger_weight.shape
    half = depth // 2
    me = lax.axis_index("dp").astype(jnp.uint32)
    first_core = (me & 1) == 0
    first_group = lax.axis_index("groups") == 0
    spot = jnp.where((me & 2) == 0, me >> 2, jnp.uint32(chips - 1) - (me >> 2))

    swap = functools.partial(lax.ppermute, axis_name="dp", perm=swap_pairs(n))
    cross = functools.partial(lax.ppermute, axis_name="groups", perm=swap_pairs(2))
    ahead = functools.partial(lax.ppermute, axis_name="dp", perm=ring_pairs(chips, 1))
    back = functools.partial(lax.ppermute, axis_name="dp", perm=ring_pairs(chips, -1))

    left = right = jnp.where(first_group, merger_weight[:half], merger_weight[half:])
    act = jax.nn.gelu(merger_input.astype(jnp.float32), approximate=False).astype(jnp.bfloat16)
    act = act.reshape(rows, chips, 2, 2, half)
    kept = jnp.where(first_core, act[:, :, 0], act[:, :, 1])
    given = jnp.where(first_core, act[:, :, 1], act[:, :, 0])
    act = jnp.concatenate([kept, swap(given)], axis=0)
    kept = jnp.where(first_group, act[:, :, 0], act[:, :, 1])
    given = jnp.where(first_group, act[:, :, 1], act[:, :, 0])
    act = jnp.concatenate([kept, cross(given)], axis=0)
    act = around(act.transpose(1, 0, 2), spot)

    def term(offset, weight, low, high):
        return jnp.dot(act[offset % chips][:, low:high], weight, preferred_element_type=jnp.float32)

    total = term(0, left, 0, half)
    for step in range(1, far):
        left = ahead(left)
        right = back(right)
        total = total + term(-step, left, 0, half) + term(step, right, 0, half)
    mid = (half + 15) // 16 * 8
    total = total + term(far, ahead(left[:mid]), 0, mid) + term(far, back(right[mid:]), mid, half)
    total = total.reshape(4, rows, width)
    theirs = (total[2] + swap(total[3])).astype(jnp.bfloat16)
    merged = total[0] + swap(total[1]) + merger_bias + cross(theirs).astype(jnp.float32)
    scale = lax.rsqrt(jnp.mean(merged * merged, axis=1, keepdims=True) + 1e-06)
    normed = (merged * scale * norm_gain).astype(jnp.bfloat16)

    counts = combine_ints.astype(jnp.float32)
    weights = counts / jnp.sum(counts, axis=1, keepdims=True)
    named = expert_ids[:, :, None] == jnp.arange(n, dtype=jnp.int32)[None, None, :]
    spread = jnp.sum(jnp.where(named, weights[:, :, None], 0.0), axis=1)
    share = lax.all_to_all(spread.T, "dp", split_axis=0, concat_axis=0, tiled=True)
    share = share.reshape(chips, 2, rows)
    share = jnp.where(first_core, share, share[:, ::-1])
    share = around(share, spot).reshape(n, rows).T

    experts = [w[0] for w in (gate_weight, up_weight, down_weight)]
    cut = rows // 2
    left = right = normed
    other = swap(normed)
    outs = [serve([normed, other], [(0, 0, rows), (1, 0, rows)], share, experts)]
    for step in range(1, far + 1):
        if step < far:
            lo, hi = 2 * (chips - step), 2 * step
            columns = [(lo, 0, rows), (hi, 0, rows), (lo + 1, 0, rows), (hi + 1, 0, rows)]
        else:
            left, right = left[:cut], right[cut:]
            lo = 2 * far
            columns = [(lo, 0, cut), (lo, cut, rows), (lo + 1, 0, cut), (lo + 1, cut, rows)]
        left = ahead(left)
        right = back(right)
        left_other, right_other = swap(left), swap(right)
        outs.append(serve([left, right, left_other, right_other], columns, share, experts))
    sums = [own.astype(jnp.float32) + swap(other).astype(jnp.float32) for own, other in outs]
    top, bottom = ahead(sums[far][:cut].astype(jnp.bfloat16)), back(sums[far][cut:].astype(jnp.bfloat16))
    top = jnp.pad(top, ((0, rows - cut), (0, 0)))
    bottom = jnp.pad(bottom, ((cut, 0), (0, 0)))
    for step in reversed(range(1, far)):
        to_back, to_ahead = sums[step][:rows], sums[step][rows:]
        top = ahead((to_ahead + top.astype(jnp.float32)).astype(jnp.bfloat16))
        bottom = back((to_back + bottom.astype(jnp.float32)).astype(jnp.bfloat16))
    combined = sums[0] + top.astype(jnp.float32) + bottom.astype(jnp.float32)
    return (merged + combined).astype(jnp.bfloat16)


def shards(*arrays):
    gate_weight, expert_ids = arrays[4], arrays[7]
    n = lax.axis_size("dp")
    rows, choose = expert_ids.shape
    capacity = (3 * rows * choose + 2 * n - 1) // (2 * n)
    if lax.axis_size("groups") == 2 and gate_weight.shape[0] == 1 and n % 4 == 0 and n >= 8 and 2 * capacity >= rows:
        return dense(*arrays)
    return routed(*arrays)


def solution(mesh):
    placed = (
        P(("groups", "dp"), None),
        P("dp", None),
        P(),
        P(),
        P("dp", None, None),
        P("dp", None, None),
        P("dp", None, None),
        P(("groups", "dp"), None),
        P(("groups", "dp"), None),
    )
    return jax.shard_map(
        shards, mesh=mesh, in_specs=placed, out_specs=P(("groups", "dp"), None), check_vma=False
    )
```

```python
import functools

import jax
import jax.numpy as jnp
from jax import lax
from jax.experimental import pallas as pl
from jax.experimental.pallas import tpu as pltpu
from jax.sharding import PartitionSpec as P


def run_experts(received, gate_weight, up_weight, down_weight, ndevices):
    local = gate_weight.shape[0]
    slots = received.shape[1]
    width = received.shape[2]
    inputs = received.reshape(ndevices, local, slots, width)
    gate = jnp.einsum("jlcd,ldh->jlch", inputs, gate_weight, preferred_element_type=jnp.float32)
    up = jnp.einsum("jlcd,ldh->jlch", inputs, up_weight, preferred_element_type=jnp.float32)
    hidden = (jax.nn.silu(gate) * up).astype(jnp.bfloat16)
    output = jnp.einsum("jlch,lhd->jlcd", hidden, down_weight, preferred_element_type=jnp.float32)
    return output.astype(jnp.bfloat16).reshape(ndevices * local, slots, width)


def routed(
    merger_input,
    merger_weight,
    merger_bias,
    norm_gain,
    gate_weight,
    up_weight,
    down_weight,
    expert_ids,
    combine_ints,
):
    ndevices = lax.axis_size("dp")
    rows = merger_input.shape[0]
    width = merger_weight.shape[1]
    choose = expert_ids.shape[1]
    experts_all = gate_weight.shape[0] * ndevices
    capacity = (3 * rows * choose + 2 * ndevices - 1) // (2 * ndevices)
    act = jax.nn.gelu(merger_input.astype(jnp.float32), approximate=False).astype(jnp.bfloat16)
    merged = jnp.dot(
        act,
        lax.all_gather(merger_weight, "dp", axis=0, tiled=True),
        preferred_element_type=jnp.float32,
    )
    merged = merged + merger_bias
    scale = lax.rsqrt(jnp.mean(merged * merged, axis=1, keepdims=True) + 1e-06)
    normed = (merged * scale * norm_gain).astype(jnp.bfloat16)
    onehot = (
        expert_ids[:, :, None] == jnp.arange(experts_all, dtype=jnp.int32)[None, None, :]
    ).astype(jnp.int32)
    flat_hot = onehot.reshape(rows * choose, experts_all)
    before = jnp.cumsum(flat_hot, axis=0) - flat_hot
    position = jnp.sum(before * flat_hot, axis=1)
    slot_flat = expert_ids.reshape(rows * choose) * capacity + position
    repeated = jnp.repeat(normed, choose, axis=0)
    outgoing = jnp.zeros((experts_all * capacity, width), jnp.bfloat16).at[slot_flat].set(repeated)
    outgoing = outgoing.reshape(experts_all, capacity, width)
    received = lax.all_to_all(outgoing, "dp", split_axis=0, concat_axis=0, tiled=True)
    served = run_experts(received, gate_weight, up_weight, down_weight, ndevices)
    returned = lax.all_to_all(served, "dp", split_axis=0, concat_axis=0, tiled=True)
    returned = returned.reshape(experts_all * capacity, width)
    picked = returned[slot_flat].reshape(rows, choose, width)
    counts = combine_ints.astype(jnp.float32)
    weights = counts / jnp.sum(counts, axis=1, keepdims=True)
    combined = jnp.sum(weights[:, :, None] * picked.astype(jnp.float32), axis=1)
    return (merged + combined).astype(jnp.bfloat16)


LANES = 128


def swap_pairs(n):
    return [(i, i ^ 1) for i in range(n)]


def ring_order(chips):
    half = chips // 2
    return [2 * z for z in range(half)] + [2 * z + 1 for z in reversed(range(half))]


def ring_pairs(chips, by):
    order = ring_order(chips)
    pairs = []
    for spot, chip in enumerate(order):
        target = order[(spot + by) % chips]
        pairs += [(2 * chip, 2 * target), (2 * chip + 1, 2 * target + 1)]
    return pairs


def tile_of(extent, most):
    return max(t for t in range(LANES, most + 1, LANES) if extent % t == 0)


def serve_body(blocks, expert_ref, *refs):
    ins = refs[:blocks]
    gate_ref, up_ref, down_ref, own_ref, other_ref, x_ref, h_ref = refs[blocks:]
    width, wide = gate_ref.shape
    start = 0
    share = []
    for ref in ins:
        size = ref.shape[0]
        x_ref[start : start + size, :] = ref[:, :width]
        tags = ref[:, width:].astype(jnp.float32)
        mine = lax.broadcasted_iota(jnp.int32, tags.shape, 1) == expert_ref[0]
        chosen = jnp.sum(jnp.where(mine, tags, 0.0), axis=1, keepdims=True)
        share.append(chosen / jnp.sum(tags, axis=1, keepdims=True))
        start += size
    share = jnp.concatenate(share, axis=0)
    tile = tile_of(wide, 256)
    for at in range(0, wide, tile):
        x = x_ref[...]
        gate = jnp.dot(x, gate_ref[:, at : at + tile], preferred_element_type=jnp.float32)
        up = jnp.dot(x, up_ref[:, at : at + tile], preferred_element_type=jnp.float32)
        h_ref[:, at : at + tile] = (gate * (1.0 / (1.0 + jnp.exp(-gate))) * up * share).astype(jnp.bfloat16)
    half = start // 2
    tile = tile_of(width, 512)
    for at in range(0, width, tile):
        out = jnp.dot(h_ref[...], down_ref[:, at : at + tile], preferred_element_type=jnp.float32)
        own_ref[:, at : at + tile] = out[:half].astype(jnp.bfloat16)
        other_ref[:, at : at + tile] = out[half:].astype(jnp.bfloat16)


VMEM = pl.BlockSpec(memory_space=pltpu.VMEM)


def serve(ins, expert, experts):
    rows = sum(x.shape[0] for x in ins)
    width, wide = experts[0].shape
    return pl.pallas_call(
        functools.partial(serve_body, len(ins)),
        out_shape=[jax.ShapeDtypeStruct((rows // 2, width), jnp.bfloat16)] * 2,
        in_specs=[pl.BlockSpec(memory_space=pltpu.SMEM)] + [VMEM] * (len(ins) + 3),
        out_specs=[VMEM, VMEM],
        scratch_shapes=[pltpu.VMEM((rows, width), jnp.bfloat16), pltpu.VMEM((rows, wide), jnp.bfloat16)],
        compiler_params=pltpu.CompilerParams(vmem_limit_bytes=VMEM_LIMIT),
        cost_estimate=pl.CostEstimate(
            flops=6 * rows * width * wide, bytes_accessed=6 * width * wide, transcendentals=rows * wide
        ),
        name="serve",
    )(expert, *ins, *experts)


def bulk_body(offsets, act_ref, *refs):
    pieces, out_ref = refs[:-1], refs[-1]
    width = out_ref.shape[1]
    tile = tile_of(width, 512)
    for at in range(0, width, tile):
        total = None
        for offset, piece in zip(offsets, pieces):
            part = jnp.dot(act_ref[offset], piece[:, at : at + tile], preferred_element_type=jnp.float32)
            total = part if total is None else total + part
        out_ref[:, at : at + tile] = total


def bulk(act, offsets, pieces):
    shape = (act.shape[1], pieces[0].shape[1])
    depth = sum(piece.shape[0] for piece in pieces)
    return pl.pallas_call(
        functools.partial(bulk_body, offsets),
        out_shape=jax.ShapeDtypeStruct(shape, jnp.float32),
        in_specs=[VMEM] * (len(pieces) + 1),
        out_specs=VMEM,
        compiler_params=pltpu.CompilerParams(vmem_limit_bytes=VMEM_LIMIT),
        cost_estimate=pl.CostEstimate(
            flops=2 * shape[0] * shape[1] * depth, bytes_accessed=4 * shape[0] * shape[1], transcendentals=0
        ),
        name="bulk",
    )(act, *pieces)


def last_body(far, act_ref, total_ref, top_ref, bottom_ref, *outs):
    width = total_ref.shape[1]
    mid = top_ref.shape[0]
    rows = outs[0].shape[0]
    tile = tile_of(width, 512)
    for at in range(0, width, tile):
        to = at + tile
        total = total_ref[:, at:to]
        total += jnp.dot(act_ref[far][:, :mid], top_ref[:, at:to], preferred_element_type=jnp.float32)
        total += jnp.dot(act_ref[far][:, mid:], bottom_ref[:, at:to], preferred_element_type=jnp.float32)
        for index, out in enumerate(outs):
            out[:, at:to] = total[index * rows : (index + 1) * rows]


def last(act, far, total, top, bottom):
    rows, width = total.shape
    return pl.pallas_call(
        functools.partial(last_body, far),
        out_shape=[jax.ShapeDtypeStruct((rows // 4, width), jnp.float32)] * 4,
        in_specs=[VMEM] * 4,
        out_specs=[VMEM] * 4,
        compiler_params=pltpu.CompilerParams(vmem_limit_bytes=VMEM_LIMIT),
        cost_estimate=pl.CostEstimate(
            flops=2 * rows * width * act.shape[2], bytes_accessed=8 * rows * width, transcendentals=0
        ),
        name="last",
    )(act, total, top, bottom)


def norm_body(parts, *refs):
    bias_ref, gain_ref, tags_ref, merged_ref, block_ref = refs[3 * parts :]
    width = merged_ref.shape[1]
    at = 0
    square = 0.0
    for index in range(parts):
        own_ref, other_ref, cross_ref = refs[3 * index : 3 * index + 3]
        to = at + own_ref.shape[1]
        merged = own_ref[...] + other_ref[...] + bias_ref[:, at:to] + cross_ref[...].astype(jnp.float32)
        merged_ref[:, at:to] = merged
        square += jnp.sum(merged * merged, axis=1, keepdims=True)
        at = to
    scale = lax.rsqrt(square / width + 1e-06)
    block_ref[:, :width] = (merged_ref[...] * scale * gain_ref[...]).astype(jnp.bfloat16)
    block_ref[:, width:] = tags_ref[...]


def normalize(parts, bias, gain, tags):
    rows = tags.shape[0]
    width = bias.shape[0]
    flat = [array for part in parts for array in part]
    return pl.pallas_call(
        functools.partial(norm_body, len(parts)),
        out_shape=[
            jax.ShapeDtypeStruct((rows, width), jnp.float32),
            jax.ShapeDtypeStruct((rows, width + tags.shape[1]), jnp.bfloat16),
        ],
        in_specs=[VMEM] * (len(flat) + 3),
        out_specs=[VMEM, VMEM],
        compiler_params=pltpu.CompilerParams(vmem_limit_bytes=VMEM_LIMIT),
        name="normalize",
    )(*flat, bias[None], gain[None], tags)


VMEM_LIMIT = 24 * 1024 * 1024
PARTS = 2


def add_body(at, own_ref, other_ref, *refs):
    out_ref = refs[-1]
    size = out_ref.shape[0]
    total = own_ref[at : at + size, :].astype(jnp.float32) + other_ref[at : at + size, :].astype(jnp.float32)
    for ref in refs[:-1]:
        total += ref[...].astype(jnp.float32)
    out_ref[...] = total.astype(jnp.bfloat16)


def add(own, other, at, size, total):
    ins = [own, other] + ([] if total is None else [total])
    return pl.pallas_call(
        functools.partial(add_body, at),
        out_shape=jax.ShapeDtypeStruct((size, own.shape[1]), jnp.bfloat16),
        in_specs=[VMEM] * len(ins),
        out_specs=VMEM,
        compiler_params=pltpu.CompilerParams(vmem_limit_bytes=VMEM_LIMIT),
        name="add",
    )(*ins)


def finish_body(merged_ref, own_ref, other_ref, *refs):
    out_ref = refs[-1]
    at = 0
    for index in range(0, len(refs) - 1, 2):
        first, second = refs[index], refs[index + 1]
        to = at + first.shape[0]
        total = own_ref[at:to, :].astype(jnp.float32) + other_ref[at:to, :].astype(jnp.float32)
        total += first[...].astype(jnp.float32) + second[...].astype(jnp.float32)
        out_ref[at:to, :] = (merged_ref[at:to, :] + total).astype(jnp.bfloat16)
        at = to


def finish(merged, *ins):
    return pl.pallas_call(
        finish_body,
        out_shape=jax.ShapeDtypeStruct(merged.shape, jnp.bfloat16),
        in_specs=[VMEM] * (len(ins) + 1),
        out_specs=VMEM,
        compiler_params=pltpu.CompilerParams(vmem_limit_bytes=VMEM_LIMIT),
        name="finish",
    )(merged, *ins)


def around(array, spot):
    ring = [array[0::2], array[1::2][::-1]] * 2
    zero = jnp.uint32(0)
    return lax.dynamic_slice(jnp.concatenate(ring), (spot,) + (zero,) * (array.ndim - 1), array.shape)


def dense(
    merger_input,
    merger_weight,
    merger_bias,
    norm_gain,
    gate_weight,
    up_weight,
    down_weight,
    expert_ids,
    combine_ints,
):
    n = lax.axis_size("dp")
    chips = n // 2
    far = chips // 2
    rows = merger_input.shape[0]
    depth, width = merger_weight.shape
    half = depth // 2
    me = lax.axis_index("dp").astype(jnp.uint32)
    first_core = (me & 1) == 0
    first_group = lax.axis_index("groups") == 0
    spot = jnp.where((me & 2) == 0, me >> 2, jnp.uint32(chips - 1) - (me >> 2))

    swap = functools.partial(lax.ppermute, axis_name="dp", perm=swap_pairs(n))
    cross = functools.partial(lax.ppermute, axis_name="groups", perm=swap_pairs(2))
    ahead = functools.partial(lax.ppermute, axis_name="dp", perm=ring_pairs(chips, 1))
    back = functools.partial(lax.ppermute, axis_name="dp", perm=ring_pairs(chips, -1))

    weight = jnp.where(first_group, merger_weight[:half], merger_weight[half:])
    act = jax.nn.gelu(merger_input.astype(jnp.float32), approximate=False).astype(jnp.bfloat16)
    act = act.reshape(rows, chips, 2, 2, half)
    kept = jnp.where(first_core, act[:, :, 0], act[:, :, 1])
    given = jnp.where(first_core, act[:, :, 1], act[:, :, 0])
    act = jnp.concatenate([kept, swap(given)], axis=0)
    kept = jnp.where(first_group, act[:, :, 0], act[:, :, 1])
    given = jnp.where(first_group, act[:, :, 1], act[:, :, 0])
    act = jnp.concatenate([kept, cross(given)], axis=0)
    act = around(act.transpose(1, 0, 2), spot)

    lanes = jnp.arange(-(-n // LANES) * LANES, dtype=jnp.int32)
    named = expert_ids[:, :, None] == lanes[None, None, :]
    tags = jnp.sum(jnp.where(named, combine_ints[:, :, None], 0), axis=1).astype(jnp.bfloat16)

    mid = (half + 15) // 16 * 8
    streams = []
    for part in range(PARTS):
        left = right = weight[:, part * width // PARTS : (part + 1) * width // PARTS]
        offsets, pieces = [0], [left]
        for step in range(1, far):
            left = ahead(left)
            right = back(right)
            offsets += [chips - step, step]
            pieces += [left, right]
        top = ahead(left[:mid])
        bottom = back(right[mid:])
        total = bulk(act, offsets, pieces)
        own, own_other, theirs, theirs_other = last(act, far, total, top, bottom)
        theirs = (theirs + swap(theirs_other)).astype(jnp.bfloat16)
        streams.append((own, swap(own_other), cross(theirs)))
    merged, block = normalize(streams, merger_bias, norm_gain, tags)

    experts = [w[0] for w in (gate_weight, up_weight, down_weight)]
    expert = me.astype(jnp.int32)[None]
    cut = rows // 2
    left = right = block
    other = swap(block)
    outs = [serve([block, other], expert, experts)]
    for step in range(1, far + 1):
        if step == far:
            left, right = left[:cut], right[cut:]
        left = ahead(left)
        right = back(right)
        others = swap(left), swap(right)
        outs.append(serve([left, right, *others], expert, experts))
    outs = [(own, swap(other)) for own, other in outs]

    def home(way, at, low, total):
        for step in reversed(range(1, far)):
            total = add(*outs[step], at + low, cut, total)
            total = way(total)
        return total

    ahead_high = home(ahead, rows, cut, None)
    back_low = home(back, 0, 0, None)
    ahead_low = home(ahead, rows, 0, ahead(add(*outs[far], 0, cut, None)))
    back_high = home(back, 0, cut, back(add(*outs[far], cut, cut, None)))
    return finish(merged, *outs[0], ahead_low, back_low, ahead_high, back_high)


def shards(*arrays):
    gate_weight, expert_ids = arrays[4], arrays[7]
    n = lax.axis_size("dp")
    rows, choose = expert_ids.shape
    capacity = (3 * rows * choose + 2 * n - 1) // (2 * n)
    if lax.axis_size("groups") == 2 and gate_weight.shape[0] == 1 and n % 4 == 0 and n >= 8 and 2 * capacity >= rows:
        return dense(*arrays)
    return routed(*arrays)


def solution(mesh):
    placed = (
        P(("groups", "dp"), None),
        P("dp", None),
        P(),
        P(),
        P("dp", None, None),
        P("dp", None, None),
        P("dp", None, None),
        P(("groups", "dp"), None),
        P(("groups", "dp"), None),
    )
    return jax.shard_map(
        shards, mesh=mesh, in_specs=placed, out_specs=P(("groups", "dp"), None), check_vma=False
    )
```

```python
import functools

import jax
import jax.numpy as jnp
from jax import lax
from jax.experimental import pallas as pl
from jax.experimental.pallas import tpu as pltpu
from jax.sharding import PartitionSpec as P


def run_experts(received, gate_weight, up_weight, down_weight, ndevices):
    local = gate_weight.shape[0]
    slots = received.shape[1]
    width = received.shape[2]
    inputs = received.reshape(ndevices, local, slots, width)
    gate = jnp.einsum("jlcd,ldh->jlch", inputs, gate_weight, preferred_element_type=jnp.float32)
    up = jnp.einsum("jlcd,ldh->jlch", inputs, up_weight, preferred_element_type=jnp.float32)
    hidden = (jax.nn.silu(gate) * up).astype(jnp.bfloat16)
    output = jnp.einsum("jlch,lhd->jlcd", hidden, down_weight, preferred_element_type=jnp.float32)
    return output.astype(jnp.bfloat16).reshape(ndevices * local, slots, width)


def routed(
    merger_input,
    merger_weight,
    merger_bias,
    norm_gain,
    gate_weight,
    up_weight,
    down_weight,
    expert_ids,
    combine_ints,
):
    ndevices = lax.axis_size("dp")
    rows = merger_input.shape[0]
    width = merger_weight.shape[1]
    choose = expert_ids.shape[1]
    experts_all = gate_weight.shape[0] * ndevices
    capacity = (3 * rows * choose + 2 * ndevices - 1) // (2 * ndevices)
    act = jax.nn.gelu(merger_input.astype(jnp.float32), approximate=False).astype(jnp.bfloat16)
    merged = jnp.dot(
        act,
        lax.all_gather(merger_weight, "dp", axis=0, tiled=True),
        preferred_element_type=jnp.float32,
    )
    merged = merged + merger_bias
    scale = lax.rsqrt(jnp.mean(merged * merged, axis=1, keepdims=True) + 1e-06)
    normed = (merged * scale * norm_gain).astype(jnp.bfloat16)
    onehot = (
        expert_ids[:, :, None] == jnp.arange(experts_all, dtype=jnp.int32)[None, None, :]
    ).astype(jnp.int32)
    flat_hot = onehot.reshape(rows * choose, experts_all)
    before = jnp.cumsum(flat_hot, axis=0) - flat_hot
    position = jnp.sum(before * flat_hot, axis=1)
    slot_flat = expert_ids.reshape(rows * choose) * capacity + position
    repeated = jnp.repeat(normed, choose, axis=0)
    outgoing = jnp.zeros((experts_all * capacity, width), jnp.bfloat16).at[slot_flat].set(repeated)
    outgoing = outgoing.reshape(experts_all, capacity, width)
    received = lax.all_to_all(outgoing, "dp", split_axis=0, concat_axis=0, tiled=True)
    served = run_experts(received, gate_weight, up_weight, down_weight, ndevices)
    returned = lax.all_to_all(served, "dp", split_axis=0, concat_axis=0, tiled=True)
    returned = returned.reshape(experts_all * capacity, width)
    picked = returned[slot_flat].reshape(rows, choose, width)
    counts = combine_ints.astype(jnp.float32)
    weights = counts / jnp.sum(counts, axis=1, keepdims=True)
    combined = jnp.sum(weights[:, :, None] * picked.astype(jnp.float32), axis=1)
    return (merged + combined).astype(jnp.bfloat16)


LANES = 128


def swap_pairs(n):
    return [(i, i ^ 1) for i in range(n)]


def ring_order(chips):
    half = chips // 2
    return [2 * z for z in range(half)] + [2 * z + 1 for z in reversed(range(half))]


def ring_pairs(chips, by):
    order = ring_order(chips)
    pairs = []
    for spot, chip in enumerate(order):
        target = order[(spot + by) % chips]
        pairs += [(2 * chip, 2 * target), (2 * chip + 1, 2 * target + 1)]
    return pairs


def tile_of(extent, most):
    return max(t for t in range(LANES, most + 1, LANES) if extent % t == 0)


def serve_body(columns, share_ref, *refs):
    blocks = len(columns)
    ins = refs[:blocks]
    gate_ref, up_ref, down_ref, own_ref, other_ref, x_ref, h_ref = refs[blocks:]
    width, wide = gate_ref.shape
    start = 0
    share = []
    for ref, (column, low, high) in zip(ins, columns):
        x_ref[start : start + high - low, :] = ref[...]
        share.append(share_ref[low:high, column : column + 1])
        start += high - low
    share = jnp.concatenate(share, axis=0)
    tile = tile_of(wide, 256)
    for at in range(0, wide, tile):
        x = x_ref[...]
        gate = jnp.dot(x, gate_ref[:, at : at + tile], preferred_element_type=jnp.float32)
        up = jnp.dot(x, up_ref[:, at : at + tile], preferred_element_type=jnp.float32)
        h_ref[:, at : at + tile] = (gate * (1.0 / (1.0 + jnp.exp(-gate))) * up * share).astype(jnp.bfloat16)
    half = start // 2
    tile = tile_of(width, 512)
    for at in range(0, width, tile):
        out = jnp.dot(h_ref[...], down_ref[:, at : at + tile], preferred_element_type=jnp.float32)
        own_ref[:, at : at + tile] = out[:half].astype(jnp.bfloat16)
        other_ref[:, at : at + tile] = out[half:].astype(jnp.bfloat16)


VMEM = pl.BlockSpec(memory_space=pltpu.VMEM)


def serve(ins, columns, share, experts):
    rows = sum(x.shape[0] for x in ins)
    width, wide = experts[0].shape
    return pl.pallas_call(
        functools.partial(serve_body, columns),
        out_shape=[jax.ShapeDtypeStruct((rows // 2, width), jnp.bfloat16)] * 2,
        in_specs=[VMEM] * (len(ins) + 4),
        out_specs=[VMEM, VMEM],
        scratch_shapes=[pltpu.VMEM((rows, width), jnp.bfloat16), pltpu.VMEM((rows, wide), jnp.bfloat16)],
        compiler_params=pltpu.CompilerParams(vmem_limit_bytes=VMEM_LIMIT),
        cost_estimate=pl.CostEstimate(
            flops=6 * rows * width * wide, bytes_accessed=6 * width * wide, transcendentals=rows * wide
        ),
        name="serve",
    )(share, *ins, *experts)


def bulk_body(offsets, act_ref, *refs):
    pieces, out_ref = refs[:-1], refs[-1]
    width = out_ref.shape[1]
    tile = tile_of(width, 512)
    for at in range(0, width, tile):
        total = None
        for offset, piece in zip(offsets, pieces):
            part = jnp.dot(act_ref[offset], piece[:, at : at + tile], preferred_element_type=jnp.float32)
            total = part if total is None else total + part
        out_ref[:, at : at + tile] = total


def bulk(act, offsets, pieces):
    shape = (act.shape[1], pieces[0].shape[1])
    depth = sum(piece.shape[0] for piece in pieces)
    return pl.pallas_call(
        functools.partial(bulk_body, offsets),
        out_shape=jax.ShapeDtypeStruct(shape, jnp.float32),
        in_specs=[VMEM] * (len(pieces) + 1),
        out_specs=VMEM,
        compiler_params=pltpu.CompilerParams(vmem_limit_bytes=VMEM_LIMIT),
        cost_estimate=pl.CostEstimate(
            flops=2 * shape[0] * shape[1] * depth, bytes_accessed=4 * shape[0] * shape[1], transcendentals=0
        ),
        name="bulk",
    )(act, *pieces)


def last_body(far, act_ref, total_ref, top_ref, bottom_ref, *outs):
    width = total_ref.shape[1]
    mid = top_ref.shape[0]
    rows = outs[0].shape[0]
    tile = tile_of(width, 512)
    for at in range(0, width, tile):
        to = at + tile
        total = total_ref[:, at:to]
        total += jnp.dot(act_ref[far][:, :mid], top_ref[:, at:to], preferred_element_type=jnp.float32)
        total += jnp.dot(act_ref[far][:, mid:], bottom_ref[:, at:to], preferred_element_type=jnp.float32)
        for index, out in enumerate(outs):
            out[:, at:to] = total[index * rows : (index + 1) * rows]


def last(act, far, total, top, bottom):
    rows, width = total.shape
    return pl.pallas_call(
        functools.partial(last_body, far),
        out_shape=[jax.ShapeDtypeStruct((rows // 4, width), jnp.float32)] * 4,
        in_specs=[VMEM] * 4,
        out_specs=[VMEM] * 4,
        compiler_params=pltpu.CompilerParams(vmem_limit_bytes=VMEM_LIMIT),
        cost_estimate=pl.CostEstimate(
            flops=2 * rows * width * act.shape[2], bytes_accessed=8 * rows * width, transcendentals=0
        ),
        name="last",
    )(act, total, top, bottom)


def norm_body(parts, *refs):
    bias_ref, gain_ref, merged_ref, low_ref, high_ref = refs[3 * parts :]
    width = merged_ref.shape[1]
    cut = low_ref.shape[0]
    at = 0
    square = 0.0
    for index in range(parts):
        own_ref, other_ref, cross_ref = refs[3 * index : 3 * index + 3]
        to = at + own_ref.shape[1]
        merged = own_ref[...] + other_ref[...] + bias_ref[:, at:to] + cross_ref[...].astype(jnp.float32)
        merged_ref[:, at:to] = merged
        square += jnp.sum(merged * merged, axis=1, keepdims=True)
        at = to
    scale = lax.rsqrt(square / width + 1e-06)
    low_ref[...] = (merged_ref[:cut, :] * scale[:cut] * gain_ref[...]).astype(jnp.bfloat16)
    high_ref[...] = (merged_ref[cut:, :] * scale[cut:] * gain_ref[...]).astype(jnp.bfloat16)


def normalize(parts, bias, gain):
    rows = parts[0][0].shape[0]
    width = bias.shape[0]
    flat = [array for part in parts for array in part]
    half = jax.ShapeDtypeStruct((rows // 2, width), jnp.bfloat16)
    return pl.pallas_call(
        functools.partial(norm_body, len(parts)),
        out_shape=[jax.ShapeDtypeStruct((rows, width), jnp.float32), half, half],
        in_specs=[VMEM] * (len(flat) + 2),
        out_specs=[VMEM] * 3,
        compiler_params=pltpu.CompilerParams(vmem_limit_bytes=VMEM_LIMIT),
        name="normalize",
    )(*flat, bias[None], gain[None])


VMEM_LIMIT = 24 * 1024 * 1024
PARTS = 2


def add_body(at, own_ref, other_ref, *refs):
    out_ref = refs[-1]
    size = out_ref.shape[0]
    total = own_ref[at : at + size, :].astype(jnp.float32) + other_ref[at : at + size, :].astype(jnp.float32)
    for ref in refs[:-1]:
        total += ref[...].astype(jnp.float32)
    out_ref[...] = total.astype(jnp.bfloat16)


def add(own, other, at, size, total):
    ins = [own, other] + ([] if total is None else [total])
    return pl.pallas_call(
        functools.partial(add_body, at),
        out_shape=jax.ShapeDtypeStruct((size, own.shape[1]), jnp.bfloat16),
        in_specs=[VMEM] * len(ins),
        out_specs=VMEM,
        compiler_params=pltpu.CompilerParams(vmem_limit_bytes=VMEM_LIMIT),
        name="add",
    )(*ins)


def finish_body(merged_ref, *refs):
    out_ref = refs[-1]
    at = 0
    for index in range(0, len(refs) - 1, 4):
        ins = refs[index : index + 4]
        to = at + ins[0].shape[0]
        total = sum(ref[...].astype(jnp.float32) for ref in ins)
        out_ref[at:to, :] = (merged_ref[at:to, :] + total).astype(jnp.bfloat16)
        at = to


def finish(merged, *ins):
    return pl.pallas_call(
        finish_body,
        out_shape=jax.ShapeDtypeStruct(merged.shape, jnp.bfloat16),
        in_specs=[VMEM] * (len(ins) + 1),
        out_specs=VMEM,
        compiler_params=pltpu.CompilerParams(vmem_limit_bytes=VMEM_LIMIT),
        name="finish",
    )(merged, *ins)


def around(array, spot):
    ring = [array[0::2], array[1::2][::-1]] * 2
    zero = jnp.uint32(0)
    return lax.dynamic_slice(jnp.concatenate(ring), (spot,) + (zero,) * (array.ndim - 1), array.shape)


def dense(
    merger_input,
    merger_weight,
    merger_bias,
    norm_gain,
    gate_weight,
    up_weight,
    down_weight,
    expert_ids,
    combine_ints,
):
    n = lax.axis_size("dp")
    chips = n // 2
    far = chips // 2
    rows = merger_input.shape[0]
    depth, width = merger_weight.shape
    half = depth // 2
    me = lax.axis_index("dp").astype(jnp.uint32)
    first_core = (me & 1) == 0
    first_group = lax.axis_index("groups") == 0
    spot = jnp.where((me & 2) == 0, me >> 2, jnp.uint32(chips - 1) - (me >> 2))

    swap = functools.partial(lax.ppermute, axis_name="dp", perm=swap_pairs(n))
    cross = functools.partial(lax.ppermute, axis_name="groups", perm=swap_pairs(2))
    ahead = functools.partial(lax.ppermute, axis_name="dp", perm=ring_pairs(chips, 1))
    back = functools.partial(lax.ppermute, axis_name="dp", perm=ring_pairs(chips, -1))

    weight = jnp.where(first_group, merger_weight[:half], merger_weight[half:])
    act = jax.nn.gelu(merger_input.astype(jnp.float32), approximate=False).astype(jnp.bfloat16)
    act = act.reshape(rows, chips, 2, 2, half)
    kept = jnp.where(first_core, act[:, :, 0], act[:, :, 1])
    given = jnp.where(first_core, act[:, :, 1], act[:, :, 0])
    act = jnp.concatenate([kept, swap(given)], axis=0)
    kept = jnp.where(first_group, act[:, :, 0], act[:, :, 1])
    given = jnp.where(first_group, act[:, :, 1], act[:, :, 0])
    act = jnp.concatenate([kept, cross(given)], axis=0)
    act = around(act.transpose(1, 0, 2), spot)

    mid = (half + 15) // 16 * 8
    streams = []
    for part in range(PARTS):
        left = right = weight[:, part * width // PARTS : (part + 1) * width // PARTS]
        offsets, pieces = [0], [left]
        for step in range(1, far):
            left = ahead(left)
            right = back(right)
            offsets += [chips - step, step]
            pieces += [left, right]
        top = ahead(left[:mid])
        bottom = back(right[mid:])
        total = bulk(act, offsets, pieces)
        own, own_other, theirs, theirs_other = last(act, far, total, top, bottom)
        theirs = (theirs + swap(theirs_other)).astype(jnp.bfloat16)
        theirs = cross(theirs)
        streams.append((own, swap(own_other), theirs))
    merged, *block = normalize(streams, merger_bias, norm_gain)

    counts = combine_ints.astype(jnp.float32)
    weights = counts / jnp.sum(counts, axis=1, keepdims=True)
    named = expert_ids[:, :, None] == jnp.arange(n, dtype=jnp.int32)[None, None, :]
    spread = jnp.sum(jnp.where(named, weights[:, :, None], 0.0), axis=1)
    share = lax.all_to_all(spread.T, "dp", split_axis=0, concat_axis=0, tiled=True)
    share = share.reshape(chips, 2, rows)
    share = jnp.where(first_core, share, share[:, ::-1])
    share = around(share, spot).reshape(n, rows).T

    experts = [w[0] for w in (gate_weight, up_weight, down_weight)]
    cut = rows // 2
    spans = [(0, cut), (cut, rows)]
    outs = []
    left, right = list(block), list(block)
    for half, span in enumerate(spans):
        outs.append([serve([block[half], swap(block[half])], [(0, *span), (1, *span)], share, experts)])
    for step in range(1, far):
        lo, hi = 2 * (chips - step), 2 * step
        for half, span in enumerate(spans):
            left[half] = ahead(left[half])
            right[half] = back(right[half])
            others = swap(left[half]), swap(right[half])
            columns = [(lo, *span), (hi, *span), (lo + 1, *span), (hi + 1, *span)]
            outs[half].append(serve([left[half], right[half], *others], columns, share, experts))
    top = ahead(left[0])
    bottom = back(right[1])
    columns = [(2 * far + side, *span) for side in (0, 1) for span in spans]
    distant = serve([top, bottom, swap(top), swap(bottom)], columns, share, experts)
    distant = (distant[0], swap(distant[1]))
    outs = [[(own, swap(other)) for own, other in pairs] for pairs in outs]

    def home(way, half, at, total):
        for step in reversed(range(1, far)):
            total = add(*outs[half][step], at, cut, total)
            total = way(total)
        return total

    ahead_high = home(ahead, 1, cut, None)
    back_low = home(back, 0, 0, None)
    ahead_low = home(ahead, 0, cut, ahead(add(*distant, 0, cut, None)))
    back_high = home(back, 1, 0, back(add(*distant, cut, cut, None)))
    return finish(merged, *outs[0][0], ahead_low, back_low, *outs[1][0], ahead_high, back_high)


def shards(*arrays):
    gate_weight, expert_ids = arrays[4], arrays[7]
    n = lax.axis_size("dp")
    rows, choose = expert_ids.shape
    capacity = (3 * rows * choose + 2 * n - 1) // (2 * n)
    if lax.axis_size("groups") == 2 and gate_weight.shape[0] == 1 and n % 4 == 0 and n >= 8 and 2 * capacity >= rows:
        return dense(*arrays)
    return routed(*arrays)


def solution(mesh):
    placed = (
        P(("groups", "dp"), None),
        P("dp", None),
        P(),
        P(),
        P("dp", None, None),
        P("dp", None, None),
        P("dp", None, None),
        P(("groups", "dp"), None),
        P(("groups", "dp"), None),
    )
    return jax.shard_map(
        shards, mesh=mesh, in_specs=placed, out_specs=P(("groups", "dp"), None), check_vma=False
    )
```

```python
import functools

import jax
import jax.numpy as jnp
from jax import lax
from jax.experimental import pallas as pl
from jax.experimental.pallas import tpu as pltpu
from jax.sharding import PartitionSpec as P


def run_experts(received, gate_weight, up_weight, down_weight, ndevices):
    local = gate_weight.shape[0]
    slots = received.shape[1]
    width = received.shape[2]
    inputs = received.reshape(ndevices, local, slots, width)
    gate = jnp.einsum("jlcd,ldh->jlch", inputs, gate_weight, preferred_element_type=jnp.float32)
    up = jnp.einsum("jlcd,ldh->jlch", inputs, up_weight, preferred_element_type=jnp.float32)
    hidden = (jax.nn.silu(gate) * up).astype(jnp.bfloat16)
    output = jnp.einsum("jlch,lhd->jlcd", hidden, down_weight, preferred_element_type=jnp.float32)
    return output.astype(jnp.bfloat16).reshape(ndevices * local, slots, width)


def routed(
    merger_input,
    merger_weight,
    merger_bias,
    norm_gain,
    gate_weight,
    up_weight,
    down_weight,
    expert_ids,
    combine_ints,
):
    ndevices = lax.axis_size("dp")
    rows = merger_input.shape[0]
    width = merger_weight.shape[1]
    choose = expert_ids.shape[1]
    experts_all = gate_weight.shape[0] * ndevices
    capacity = (3 * rows * choose + 2 * ndevices - 1) // (2 * ndevices)
    act = jax.nn.gelu(merger_input.astype(jnp.float32), approximate=False).astype(jnp.bfloat16)
    merged = jnp.dot(
        act,
        lax.all_gather(merger_weight, "dp", axis=0, tiled=True),
        preferred_element_type=jnp.float32,
    )
    merged = merged + merger_bias
    scale = lax.rsqrt(jnp.mean(merged * merged, axis=1, keepdims=True) + 1e-06)
    normed = (merged * scale * norm_gain).astype(jnp.bfloat16)
    onehot = (
        expert_ids[:, :, None] == jnp.arange(experts_all, dtype=jnp.int32)[None, None, :]
    ).astype(jnp.int32)
    flat_hot = onehot.reshape(rows * choose, experts_all)
    before = jnp.cumsum(flat_hot, axis=0) - flat_hot
    position = jnp.sum(before * flat_hot, axis=1)
    slot_flat = expert_ids.reshape(rows * choose) * capacity + position
    repeated = jnp.repeat(normed, choose, axis=0)
    outgoing = jnp.zeros((experts_all * capacity, width), jnp.bfloat16).at[slot_flat].set(repeated)
    outgoing = outgoing.reshape(experts_all, capacity, width)
    received = lax.all_to_all(outgoing, "dp", split_axis=0, concat_axis=0, tiled=True)
    served = run_experts(received, gate_weight, up_weight, down_weight, ndevices)
    returned = lax.all_to_all(served, "dp", split_axis=0, concat_axis=0, tiled=True)
    returned = returned.reshape(experts_all * capacity, width)
    picked = returned[slot_flat].reshape(rows, choose, width)
    counts = combine_ints.astype(jnp.float32)
    weights = counts / jnp.sum(counts, axis=1, keepdims=True)
    combined = jnp.sum(weights[:, :, None] * picked.astype(jnp.float32), axis=1)
    return (merged + combined).astype(jnp.bfloat16)


LANES = 128


def swap_pairs(n):
    return [(i, i ^ 1) for i in range(n)]


def ring_order(chips):
    half = chips // 2
    return [2 * z for z in range(half)] + [2 * z + 1 for z in reversed(range(half))]


def ring_pairs(chips, by):
    order = ring_order(chips)
    pairs = []
    for spot, chip in enumerate(order):
        target = order[(spot + by) % chips]
        pairs += [(2 * chip, 2 * target), (2 * chip + 1, 2 * target + 1)]
    return pairs


def tile_of(extent, most):
    return max(t for t in range(LANES, most + 1, LANES) if extent % t == 0)


def serve_body(blocks, expert_ref, *refs):
    ins = refs[:blocks]
    gate_ref, up_ref, down_ref, own_ref, other_ref, x_ref, h_ref = refs[blocks:]
    width, wide = gate_ref.shape
    start = 0
    share = []
    for ref in ins:
        size = ref.shape[0]
        x_ref[start : start + size, :] = ref[:, :width]
        tags = ref[:, width:].astype(jnp.float32)
        mine = lax.broadcasted_iota(jnp.int32, tags.shape, 1) == expert_ref[0]
        chosen = jnp.sum(jnp.where(mine, tags, 0.0), axis=1, keepdims=True)
        share.append(chosen / jnp.sum(tags, axis=1, keepdims=True))
        start += size
    share = jnp.concatenate(share, axis=0)
    tile = tile_of(wide, 256)
    for at in range(0, wide, tile):
        x = x_ref[...]
        gate = jnp.dot(x, gate_ref[:, at : at + tile], preferred_element_type=jnp.float32)
        up = jnp.dot(x, up_ref[:, at : at + tile], preferred_element_type=jnp.float32)
        h_ref[:, at : at + tile] = (gate * (1.0 / (1.0 + jnp.exp(-gate))) * up * share).astype(jnp.bfloat16)
    half = start // 2
    tile = tile_of(width, 512)
    for at in range(0, width, tile):
        out = jnp.dot(h_ref[...], down_ref[:, at : at + tile], preferred_element_type=jnp.float32)
        own_ref[:, at : at + tile] = out[:half].astype(jnp.bfloat16)
        other_ref[:, at : at + tile] = out[half:].astype(jnp.bfloat16)


VMEM = pl.BlockSpec(memory_space=pltpu.VMEM)


def serve(ins, expert, experts):
    rows = sum(x.shape[0] for x in ins)
    width, wide = experts[0].shape
    return pl.pallas_call(
        functools.partial(serve_body, len(ins)),
        out_shape=[jax.ShapeDtypeStruct((rows // 2, width), jnp.bfloat16)] * 2,
        in_specs=[pl.BlockSpec(memory_space=pltpu.SMEM)] + [VMEM] * (len(ins) + 3),
        out_specs=[VMEM, VMEM],
        scratch_shapes=[pltpu.VMEM((rows, width), jnp.bfloat16), pltpu.VMEM((rows, wide), jnp.bfloat16)],
        compiler_params=pltpu.CompilerParams(vmem_limit_bytes=VMEM_LIMIT),
        cost_estimate=pl.CostEstimate(
            flops=6 * rows * width * wide, bytes_accessed=6 * width * wide, transcendentals=rows * wide
        ),
        name="serve",
    )(expert, *ins, *experts)


def bulk_body(offsets, act_ref, *refs):
    pieces, out_ref = refs[:-1], refs[-1]
    width = out_ref.shape[1]
    tile = tile_of(width, 512)
    for at in range(0, width, tile):
        total = None
        for offset, piece in zip(offsets, pieces):
            part = jnp.dot(act_ref[offset], piece[:, at : at + tile], preferred_element_type=jnp.float32)
            total = part if total is None else total + part
        out_ref[:, at : at + tile] = total


def bulk(act, offsets, pieces):
    shape = (act.shape[1], pieces[0].shape[1])
    depth = sum(piece.shape[0] for piece in pieces)
    return pl.pallas_call(
        functools.partial(bulk_body, offsets),
        out_shape=jax.ShapeDtypeStruct(shape, jnp.float32),
        in_specs=[VMEM] * (len(pieces) + 1),
        out_specs=VMEM,
        compiler_params=pltpu.CompilerParams(vmem_limit_bytes=VMEM_LIMIT),
        cost_estimate=pl.CostEstimate(
            flops=2 * shape[0] * shape[1] * depth, bytes_accessed=4 * shape[0] * shape[1], transcendentals=0
        ),
        name="bulk",
    )(act, *pieces)


def last_body(far, act_ref, total_ref, top_ref, bottom_ref, *outs):
    width = total_ref.shape[1]
    mid = top_ref.shape[0]
    rows = outs[0].shape[0]
    tile = tile_of(width, 512)
    for at in range(0, width, tile):
        to = at + tile
        total = total_ref[:, at:to]
        total += jnp.dot(act_ref[far][:, :mid], top_ref[:, at:to], preferred_element_type=jnp.float32)
        total += jnp.dot(act_ref[far][:, mid:], bottom_ref[:, at:to], preferred_element_type=jnp.float32)
        for index, out in enumerate(outs):
            out[:, at:to] = total[index * rows : (index + 1) * rows]


def last(act, far, total, top, bottom):
    rows, width = total.shape
    return pl.pallas_call(
        functools.partial(last_body, far),
        out_shape=[jax.ShapeDtypeStruct((rows // 4, width), jnp.float32)] * 4,
        in_specs=[VMEM] * 4,
        out_specs=[VMEM] * 4,
        compiler_params=pltpu.CompilerParams(vmem_limit_bytes=VMEM_LIMIT),
        cost_estimate=pl.CostEstimate(
            flops=2 * rows * width * act.shape[2], bytes_accessed=8 * rows * width, transcendentals=0
        ),
        name="last",
    )(act, total, top, bottom)


def norm_body(parts, *refs):
    bias_ref, gain_ref, tags_ref, merged_ref, low_ref, high_ref = refs[3 * parts :]
    width = merged_ref.shape[1]
    cut = low_ref.shape[0]
    low_ref[:, width:] = tags_ref[:cut, :]
    high_ref[:, width:] = tags_ref[cut:, :]
    at = 0
    square = 0.0
    for index in range(parts):
        own_ref, other_ref, cross_ref = refs[3 * index : 3 * index + 3]
        to = at + own_ref.shape[1]
        merged = own_ref[...] + other_ref[...] + bias_ref[:, at:to] + cross_ref[...].astype(jnp.float32)
        merged_ref[:, at:to] = merged
        square += jnp.sum(merged * merged, axis=1, keepdims=True)
        at = to
    scale = lax.rsqrt(square / width + 1e-06)
    low_ref[:, :width] = (merged_ref[:cut, :] * scale[:cut] * gain_ref[...]).astype(jnp.bfloat16)
    high_ref[:, :width] = (merged_ref[cut:, :] * scale[cut:] * gain_ref[...]).astype(jnp.bfloat16)


def normalize(parts, bias, gain, tags):
    rows = parts[0][0].shape[0]
    width = bias.shape[0]
    flat = [array for part in parts for array in part]
    half = jax.ShapeDtypeStruct((rows // 2, width + tags.shape[1]), jnp.bfloat16)
    return pl.pallas_call(
        functools.partial(norm_body, len(parts)),
        out_shape=[jax.ShapeDtypeStruct((rows, width), jnp.float32), half, half],
        in_specs=[VMEM] * (len(flat) + 3),
        out_specs=[VMEM] * 3,
        compiler_params=pltpu.CompilerParams(vmem_limit_bytes=SMALL_LIMIT),
        name="normalize",
    )(*flat, bias[None], gain[None], tags)


VMEM_LIMIT = 24 * 1024 * 1024
SMALL_LIMIT = 12 * 1024 * 1024
PARTS = 2


def add_body(at, own_ref, other_ref, *refs):
    out_ref = refs[-1]
    size = out_ref.shape[0]
    total = own_ref[at : at + size, :].astype(jnp.float32) + other_ref[at : at + size, :].astype(jnp.float32)
    for ref in refs[:-1]:
        total += ref[...].astype(jnp.float32)
    out_ref[...] = total.astype(jnp.bfloat16)


def add(own, other, at, size, total):
    ins = [own, other] + ([] if total is None else [total])
    return pl.pallas_call(
        functools.partial(add_body, at),
        out_shape=jax.ShapeDtypeStruct((size, own.shape[1]), jnp.bfloat16),
        in_specs=[VMEM] * len(ins),
        out_specs=VMEM,
        compiler_params=pltpu.CompilerParams(vmem_limit_bytes=VMEM_LIMIT),
        name="add",
    )(*ins)


def finish_body(merged_ref, *refs):
    out_ref = refs[-1]
    at = 0
    for index in range(0, len(refs) - 1, 4):
        ins = refs[index : index + 4]
        to = at + ins[0].shape[0]
        total = sum(ref[...].astype(jnp.float32) for ref in ins)
        out_ref[at:to, :] = (merged_ref[at:to, :] + total).astype(jnp.bfloat16)
        at = to


def finish(merged, *ins):
    return pl.pallas_call(
        finish_body,
        out_shape=jax.ShapeDtypeStruct(merged.shape, jnp.bfloat16),
        in_specs=[VMEM] * (len(ins) + 1),
        out_specs=VMEM,
        compiler_params=pltpu.CompilerParams(vmem_limit_bytes=VMEM_LIMIT),
        name="finish",
    )(merged, *ins)


def around(array, spot):
    ring = [array[0::2], array[1::2][::-1]] * 2
    zero = jnp.uint32(0)
    return lax.dynamic_slice(jnp.concatenate(ring), (spot,) + (zero,) * (array.ndim - 1), array.shape)


def dense(
    merger_input,
    merger_weight,
    merger_bias,
    norm_gain,
    gate_weight,
    up_weight,
    down_weight,
    expert_ids,
    combine_ints,
):
    n = lax.axis_size("dp")
    chips = n // 2
    far = chips // 2
    rows = merger_input.shape[0]
    depth, width = merger_weight.shape
    half = depth // 2
    me = lax.axis_index("dp").astype(jnp.uint32)
    first_core = (me & 1) == 0
    first_group = lax.axis_index("groups") == 0
    spot = jnp.where((me & 2) == 0, me >> 2, jnp.uint32(chips - 1) - (me >> 2))

    swap = functools.partial(lax.ppermute, axis_name="dp", perm=swap_pairs(n))
    cross = functools.partial(lax.ppermute, axis_name="groups", perm=swap_pairs(2))
    ahead = functools.partial(lax.ppermute, axis_name="dp", perm=ring_pairs(chips, 1))
    back = functools.partial(lax.ppermute, axis_name="dp", perm=ring_pairs(chips, -1))

    weight = jnp.where(first_group, merger_weight[:half], merger_weight[half:])
    act = jax.nn.gelu(merger_input.astype(jnp.float32), approximate=False).astype(jnp.bfloat16)
    act = act.reshape(rows, chips, 2, 2, half)
    kept = jnp.where(first_core, act[:, :, 0], act[:, :, 1])
    given = jnp.where(first_core, act[:, :, 1], act[:, :, 0])
    given = swap(given)
    act = jnp.concatenate([kept, given], axis=0)
    kept = jnp.where(first_group, act[:, :, 0], act[:, :, 1])
    given = jnp.where(first_group, act[:, :, 1], act[:, :, 0])
    given = cross(given)
    act = jnp.concatenate([kept, given], axis=0)
    act = around(act.transpose(1, 0, 2), spot)

    mid = (half + 15) // 16 * 8
    streams = []
    for part in range(PARTS):
        left = right = weight[:, part * width // PARTS : (part + 1) * width // PARTS]
        offsets, pieces = [0], [left]
        for step in range(1, far):
            left = ahead(left)
            right = back(right)
            offsets += [chips - step, step]
            pieces += [left, right]
        top = ahead(left[:mid])
        bottom = back(right[mid:])
        total = bulk(act, offsets, pieces)
        own, own_other, theirs, theirs_other = last(act, far, total, top, bottom)
        theirs = (theirs + swap(theirs_other)).astype(jnp.bfloat16)
        theirs = cross(theirs)
        streams.append((own, swap(own_other), theirs))
    lanes = jnp.arange(-(-n // LANES) * LANES, dtype=jnp.int32)
    named = expert_ids[:, :, None] == lanes[None, None, :]
    tags = jnp.sum(jnp.where(named, combine_ints[:, :, None], 0), axis=1).astype(jnp.bfloat16)
    merged, *block = normalize(streams, merger_bias, norm_gain, tags)

    experts = [w[0] for w in (gate_weight, up_weight, down_weight)]
    cut = rows // 2
    expert = me.astype(jnp.int32)[None]
    outs = []
    left, right = list(block), list(block)
    for half in range(2):
        other = swap(block[half])
        outs.append([serve([block[half], other], expert, experts)])
    for _ in range(1, far):
        for half in range(2):
            left[half] = ahead(left[half])
            right[half] = back(right[half])
            others = swap(left[half]), swap(right[half])
            outs[half].append(serve([left[half], right[half], *others], expert, experts))
    top = ahead(left[0])
    bottom = back(right[1])
    distant = serve([top, bottom, swap(top), swap(bottom)], expert, experts)
    distant = (distant[0], swap(distant[1]))
    outs = [[(own, swap(other)) for own, other in pairs] for pairs in outs]

    def home(way, half, at, total):
        for step in reversed(range(1, far)):
            total = add(*outs[half][step], at, cut, total)
            total = way(total)
        return total

    ahead_high = home(ahead, 1, cut, None)
    back_low = home(back, 0, 0, None)
    top, bottom = add(*distant, 0, cut, None), add(*distant, cut, cut, None)
    top = ahead(top)
    bottom = back(bottom)
    ahead_low = home(ahead, 0, cut, top)
    back_high = home(back, 1, 0, bottom)
    return finish(merged, *outs[0][0], ahead_low, back_low, *outs[1][0], ahead_high, back_high)


def shards(*arrays):
    gate_weight, expert_ids = arrays[4], arrays[7]
    n = lax.axis_size("dp")
    rows, choose = expert_ids.shape
    capacity = (3 * rows * choose + 2 * n - 1) // (2 * n)
    if lax.axis_size("groups") == 2 and gate_weight.shape[0] == 1 and n % 4 == 0 and n >= 8 and 2 * capacity >= rows:
        return dense(*arrays)
    return routed(*arrays)


def solution(mesh):
    placed = (
        P(("groups", "dp"), None),
        P("dp", None),
        P(),
        P(),
        P("dp", None, None),
        P("dp", None, None),
        P("dp", None, None),
        P(("groups", "dp"), None),
        P(("groups", "dp"), None),
    )
    return jax.shard_map(
        shards, mesh=mesh, in_specs=placed, out_specs=P(("groups", "dp"), None), check_vma=False
    )
```

```python
import functools

import jax
import jax.numpy as jnp
from jax import lax
from jax.experimental import pallas as pl
from jax.experimental.pallas import tpu as pltpu
from jax.sharding import PartitionSpec as P


LANES = 128
MIB = 1024 * 1024
PARTS = 2
DP = "dp"
GROUPS = "groups"
VMEM = pl.BlockSpec(memory_space=pltpu.VMEM)


def run_experts(received, gate_weight, up_weight, down_weight, ndevices):
    local = gate_weight.shape[0]
    slots = received.shape[1]
    width = received.shape[2]
    inputs = received.reshape(ndevices, local, slots, width)
    gate = jnp.einsum("jlcd,ldh->jlch", inputs, gate_weight, preferred_element_type=jnp.float32)
    up = jnp.einsum("jlcd,ldh->jlch", inputs, up_weight, preferred_element_type=jnp.float32)
    hidden = (jax.nn.silu(gate) * up).astype(jnp.bfloat16)
    output = jnp.einsum("jlch,lhd->jlcd", hidden, down_weight, preferred_element_type=jnp.float32)
    return output.astype(jnp.bfloat16).reshape(ndevices * local, slots, width)


def routed(
    merger_input,
    merger_weight,
    merger_bias,
    norm_gain,
    gate_weight,
    up_weight,
    down_weight,
    expert_ids,
    combine_ints,
):
    ndevices = lax.axis_size("dp")
    rows = merger_input.shape[0]
    width = merger_weight.shape[1]
    choose = expert_ids.shape[1]
    experts_all = gate_weight.shape[0] * ndevices
    capacity = (3 * rows * choose + 2 * ndevices - 1) // (2 * ndevices)
    act = jax.nn.gelu(merger_input.astype(jnp.float32), approximate=False).astype(jnp.bfloat16)
    merged = jnp.dot(
        act,
        lax.all_gather(merger_weight, "dp", axis=0, tiled=True),
        preferred_element_type=jnp.float32,
    )
    merged = merged + merger_bias
    scale = lax.rsqrt(jnp.mean(merged * merged, axis=1, keepdims=True) + 1e-06)
    normed = (merged * scale * norm_gain).astype(jnp.bfloat16)
    onehot = (
        expert_ids[:, :, None] == jnp.arange(experts_all, dtype=jnp.int32)[None, None, :]
    ).astype(jnp.int32)
    flat_hot = onehot.reshape(rows * choose, experts_all)
    before = jnp.cumsum(flat_hot, axis=0) - flat_hot
    position = jnp.sum(before * flat_hot, axis=1)
    slot_flat = expert_ids.reshape(rows * choose) * capacity + position
    repeated = jnp.repeat(normed, choose, axis=0)
    outgoing = jnp.zeros((experts_all * capacity, width), jnp.bfloat16).at[slot_flat].set(repeated)
    outgoing = outgoing.reshape(experts_all, capacity, width)
    received = lax.all_to_all(outgoing, "dp", split_axis=0, concat_axis=0, tiled=True)
    served = run_experts(received, gate_weight, up_weight, down_weight, ndevices)
    returned = lax.all_to_all(served, "dp", split_axis=0, concat_axis=0, tiled=True)
    returned = returned.reshape(experts_all * capacity, width)
    picked = returned[slot_flat].reshape(rows, choose, width)
    counts = combine_ints.astype(jnp.float32)
    weights = counts / jnp.sum(counts, axis=1, keepdims=True)
    combined = jnp.sum(weights[:, :, None] * picked.astype(jnp.float32), axis=1)
    return (merged + combined).astype(jnp.bfloat16)


def swap_pairs(n):
    return [(i, i ^ 1) for i in range(n)]


def ring_order(chips):
    half = chips // 2
    return [2 * z for z in range(half)] + [2 * z + 1 for z in reversed(range(half))]


def ring_pairs(chips, by):
    order = ring_order(chips)
    pairs = []
    for spot, chip in enumerate(order):
        target = order[(spot + by) % chips]
        pairs += [(2 * chip, 2 * target), (2 * chip + 1, 2 * target + 1)]
    return pairs


def chip_at(chips, offset):
    chip = lax.axis_index(DP) // 2
    spot = jnp.where(chip % 2 == 0, chip // 2, chips - 1 - chip // 2)
    spot = lax.rem(spot + offset, chips)
    return jnp.where(spot < chips // 2, 2 * spot, 2 * (chips - 1 - spot) + 1)


def tile_of(extent, most):
    return max(t for t in range(LANES, most + 1, LANES) if extent % t == 0)


def kernel(body, outs, ins, scratch=(), limit=12 * MIB, flops=0, moved=0):
    return pl.pallas_call(
        body,
        out_shape=outs,
        in_specs=[VMEM] * len(ins),
        out_specs=jax.tree.map(lambda _: VMEM, outs),
        scratch_shapes=list(scratch),
        compiler_params=pltpu.CompilerParams(vmem_limit_bytes=limit),
        cost_estimate=pl.CostEstimate(flops=flops, bytes_accessed=moved, transcendentals=0),
    )(*ins)


def shaped(rows, width, dtype=jnp.bfloat16):
    return jax.ShapeDtypeStruct((rows, width), dtype)


def serve_body(blocks, *refs):
    ins = refs[:blocks]
    gate_ref, up_ref, down_ref, own_ref, other_ref, x_ref, h_ref = refs[blocks:]
    width, wide = gate_ref.shape
    expert = lax.axis_index(DP)
    start = 0
    share = []
    for ref in ins:
        size = ref.shape[0]
        x_ref[start : start + size, :] = ref[:, :width]
        tags = ref[:, width:].astype(jnp.float32)
        mine = lax.broadcasted_iota(jnp.int32, tags.shape, 1) == expert
        chosen = jnp.sum(jnp.where(mine, tags, 0.0), axis=1, keepdims=True)
        share.append(chosen / jnp.sum(tags, axis=1, keepdims=True))
        start += size
    share = jnp.concatenate(share, axis=0)
    tile = tile_of(wide, 256)
    for at in range(0, wide, tile):
        x = x_ref[...]
        gate = jnp.dot(x, gate_ref[:, at : at + tile], preferred_element_type=jnp.float32)
        up = jnp.dot(x, up_ref[:, at : at + tile], preferred_element_type=jnp.float32)
        h_ref[:, at : at + tile] = (gate * (1.0 / (1.0 + jnp.exp(-gate))) * up * share).astype(jnp.bfloat16)
    half = start // 2
    tile = tile_of(width, 512)
    for at in range(0, width, tile):
        out = jnp.dot(h_ref[...], down_ref[:, at : at + tile], preferred_element_type=jnp.float32)
        own_ref[:, at : at + tile] = out[:half].astype(jnp.bfloat16)
        other_ref[:, at : at + tile] = out[half:].astype(jnp.bfloat16)


def serve(ins, experts):
    rows = sum(x.shape[0] for x in ins)
    width, wide = experts[0].shape
    return kernel(
        functools.partial(serve_body, len(ins)),
        [shaped(rows // 2, width)] * 2,
        [*ins, *experts],
        [pltpu.VMEM((rows, width), jnp.bfloat16), pltpu.VMEM((rows, wide), jnp.bfloat16)],
        24 * MIB,
        6 * rows * width * wide,
        6 * width * wide,
    )


def tag_body(ids_ref, counts_ref, out_ref):
    rows, lanes = out_ref.shape
    expert = lax.broadcasted_iota(jnp.int32, (lanes, rows), 0)
    total = jnp.zeros((lanes, rows), jnp.float32)
    for k in range(ids_ref.shape[0]):
        total += jnp.where(expert == ids_ref[k : k + 1, :], counts_ref[k : k + 1, :].astype(jnp.float32), 0.0)
    out_ref[...] = total.T.astype(jnp.bfloat16)


def bulk_body(chips, offsets, act_ref, *refs):
    pieces, out_ref = refs[:-1], refs[-1]
    width = out_ref.shape[1]
    tile = tile_of(width, 512)
    for at in range(0, width, tile):
        total = None
        for offset, piece in zip(offsets, pieces):
            act = act_ref[chip_at(chips, offset)]
            part = jnp.dot(act, piece[:, at : at + tile], preferred_element_type=jnp.float32)
            total = part if total is None else total + part
        out_ref[:, at : at + tile] = total


def last_body(chips, act_ref, total_ref, top_ref, bottom_ref, *outs):
    width = total_ref.shape[1]
    mid = top_ref.shape[0]
    rows = outs[0].shape[0]
    tile = tile_of(width, 512)
    act = act_ref[chip_at(chips, chips // 2)]
    for at in range(0, width, tile):
        to = at + tile
        total = total_ref[:, at:to]
        total += jnp.dot(act[:, :mid], top_ref[:, at:to], preferred_element_type=jnp.float32)
        total += jnp.dot(act[:, mid:], bottom_ref[:, at:to], preferred_element_type=jnp.float32)
        for index, out in enumerate(outs):
            out[:, at:to] = total[index * rows : (index + 1) * rows]


def norm_body(parts, *refs):
    bias_ref, gain_ref, tags_ref, merged_ref, low_ref, high_ref = refs[3 * parts :]
    width = merged_ref.shape[1]
    cut = low_ref.shape[0]
    low_ref[:, width:] = tags_ref[:cut, :]
    high_ref[:, width:] = tags_ref[cut:, :]
    at = 0
    square = 0.0
    for index in range(parts):
        own_ref, other_ref, cross_ref = refs[3 * index : 3 * index + 3]
        to = at + own_ref.shape[1]
        merged = own_ref[...] + other_ref[...] + bias_ref[:, at:to] + cross_ref[...].astype(jnp.float32)
        merged_ref[:, at:to] = merged
        square += jnp.sum(merged * merged, axis=1, keepdims=True)
        at = to
    scale = lax.rsqrt(square / width + 1e-06)
    low_ref[:, :width] = (merged_ref[:cut, :] * scale[:cut] * gain_ref[...]).astype(jnp.bfloat16)
    high_ref[:, :width] = (merged_ref[cut:, :] * scale[cut:] * gain_ref[...]).astype(jnp.bfloat16)


def plus_body(*refs):
    refs[-1][...] = (refs[0][...] + refs[1][...]).astype(refs[-1].dtype)


def add_body(at, own_ref, other_ref, *refs):
    out_ref = refs[-1]
    size = out_ref.shape[0]
    total = own_ref[at : at + size, :].astype(jnp.float32) + other_ref[at : at + size, :].astype(jnp.float32)
    for ref in refs[:-1]:
        total += ref[...].astype(jnp.float32)
    out_ref[...] = total.astype(jnp.bfloat16)


def add(own, other, at, size, total=None):
    ins = [own, other] + ([] if total is None else [total])
    return kernel(functools.partial(add_body, at), shaped(size, own.shape[1]), ins)


def finish_body(merged_ref, *refs):
    out_ref = refs[-1]
    at = 0
    for index in range(0, len(refs) - 1, 4):
        ins = refs[index : index + 4]
        to = at + ins[0].shape[0]
        total = sum(ref[...].astype(jnp.float32) for ref in ins)
        out_ref[at:to, :] = (merged_ref[at:to, :] + total).astype(jnp.bfloat16)
        at = to


def dense(
    merger_input,
    merger_weight,
    merger_bias,
    norm_gain,
    gate_weight,
    up_weight,
    down_weight,
    expert_ids,
    combine_ints,
):
    n = lax.axis_size(DP)
    chips = n // 2
    far = chips // 2
    rows = merger_input.shape[0]
    depth, width = merger_weight.shape
    half = depth // 2
    cut = rows // 2
    first_core = lax.axis_index(DP) % 2 == 0
    first_group = lax.axis_index(GROUPS) == 0

    swap = functools.partial(lax.ppermute, axis_name=DP, perm=swap_pairs(n))
    cross = functools.partial(lax.ppermute, axis_name=GROUPS, perm=swap_pairs(2))
    rings = [functools.partial(lax.ppermute, axis_name=DP, perm=ring_pairs(chips, by)) for by in (1, -1)]

    def hop(way, array):
        return rings[way](array)

    zero = jnp.uint32(0)
    weight = lax.dynamic_slice(merger_weight, (lax.axis_index(GROUPS).astype(jnp.uint32) * half, zero), (half, width))
    act = jax.nn.gelu(merger_input.astype(jnp.float32), approximate=False).astype(jnp.bfloat16)
    act = act.reshape(rows, chips, 2, 2, half)
    kept = jnp.where(first_core, act[:, :, 0], act[:, :, 1])
    given = jnp.where(first_core, act[:, :, 1], act[:, :, 0])
    given = swap(given)
    act = jnp.concatenate([kept, given], axis=0)
    kept = jnp.where(first_group, act[:, :, 0], act[:, :, 1])
    given = jnp.where(first_group, act[:, :, 1], act[:, :, 0])
    given = cross(given)
    act = jnp.concatenate([kept, given], axis=0).transpose(1, 0, 2)

    lanes = -(-n // LANES) * LANES
    tags = kernel(tag_body, shaped(rows, lanes), [expert_ids.T, combine_ints.T])

    mid = (half + 15) // 16 * 8
    share = width // PARTS
    streams = []
    for part in range(PARTS):
        left = right = weight[:, part * share : (part + 1) * share]
        offsets, pieces = [0], [left]
        for step in range(1, far):
            left, right = hop(0, left), hop(1, right)
            offsets += [chips - step, step]
            pieces += [left, right]
        top, bottom = hop(0, left[:mid]), hop(1, right[mid:])
        size = 4 * rows * share
        total = kernel(
            functools.partial(bulk_body, chips, offsets),
            shaped(4 * rows, share, jnp.float32),
            [act, *pieces],
            flops=2 * size * half * chips,
            moved=4 * size,
        )
        own, own_other, theirs, theirs_other = kernel(
            functools.partial(last_body, chips),
            [shaped(rows, share, jnp.float32)] * 4,
            [act, total, top, bottom],
            flops=2 * size * half,
            moved=8 * size,
        )
        theirs = kernel(plus_body, shaped(rows, share), [theirs, swap(theirs_other)])
        theirs = cross(theirs)
        streams += [own, swap(own_other), theirs]
    merged, *block = kernel(
        functools.partial(norm_body, PARTS),
        [shaped(rows, width, jnp.float32)] + [shaped(cut, width + lanes)] * 2,
        [*streams, merger_bias[None], norm_gain[None], tags],
    )

    experts = [w[0] for w in (gate_weight, up_weight, down_weight)]
    arrived = [[(own,) for own in block]]
    sides = [(own, own) for own in block]
    for _ in range(1, far):
        sides = [tuple(hop(way, side[way]) for way in (0, 1)) for side in sides]
        arrived.append(sides)
    distant = hop(0, sides[0][0]), hop(1, sides[1][1])

    def served(ins):
        others = [swap(x) for x in ins]
        own, other = serve([*ins, *others], experts)
        return own, swap(other)

    outs = [[served(ins) for ins in pair] for pair in arrived]
    distant = served(distant)

    def home(way, which, at, total):
        for step in reversed(range(1, far)):
            total = add(*outs[step][which], at, cut, total)
            total = hop(way, total)
        return total

    near = home(0, 1, cut, None), home(1, 0, 0, None)
    top, bottom = (hop(way, add(*distant, way * cut, cut)) for way in (0, 1))
    top, bottom = home(0, 0, cut, top), home(1, 1, 0, bottom)
    ins = [merged, *outs[0][0], top, near[1], *outs[0][1], near[0], bottom]
    return kernel(finish_body, shaped(rows, width), ins)


def shards(*arrays):
    gate_weight, expert_ids = arrays[4], arrays[7]
    n = lax.axis_size(DP)
    rows, choose = expert_ids.shape
    capacity = (3 * rows * choose + 2 * n - 1) // (2 * n)
    if lax.axis_size(GROUPS) == 2 and gate_weight.shape[0] == 1 and n % 4 == 0 and n >= 16 and 2 * capacity >= rows:
        return dense(*arrays)
    return routed(*arrays)


def solution(mesh):
    placed = (
        P(("groups", "dp"), None),
        P("dp", None),
        P(),
        P(),
        P("dp", None, None),
        P("dp", None, None),
        P("dp", None, None),
        P(("groups", "dp"), None),
        P(("groups", "dp"), None),
    )
    return jax.shard_map(
        shards, mesh=mesh, in_specs=placed, out_specs=P(("groups", "dp"), None), check_vma=False
    )
```

```python
import functools

import jax
import jax.numpy as jnp
from jax import lax
from jax.experimental import pallas as pl
from jax.experimental.pallas import tpu as pltpu
from jax.sharding import PartitionSpec as P


LANES = 128
MIB = 1024 * 1024
PARTS = 2
DP = "dp"
GROUPS = "groups"
VMEM = pl.BlockSpec(memory_space=pltpu.VMEM)


def run_experts(received, gate_weight, up_weight, down_weight, ndevices):
    local = gate_weight.shape[0]
    slots = received.shape[1]
    width = received.shape[2]
    inputs = received.reshape(ndevices, local, slots, width)
    gate = jnp.einsum("jlcd,ldh->jlch", inputs, gate_weight, preferred_element_type=jnp.float32)
    up = jnp.einsum("jlcd,ldh->jlch", inputs, up_weight, preferred_element_type=jnp.float32)
    hidden = (jax.nn.silu(gate) * up).astype(jnp.bfloat16)
    output = jnp.einsum("jlch,lhd->jlcd", hidden, down_weight, preferred_element_type=jnp.float32)
    return output.astype(jnp.bfloat16).reshape(ndevices * local, slots, width)


def routed(
    merger_input,
    merger_weight,
    merger_bias,
    norm_gain,
    gate_weight,
    up_weight,
    down_weight,
    expert_ids,
    combine_ints,
):
    ndevices = lax.axis_size("dp")
    rows = merger_input.shape[0]
    width = merger_weight.shape[1]
    choose = expert_ids.shape[1]
    experts_all = gate_weight.shape[0] * ndevices
    capacity = (3 * rows * choose + 2 * ndevices - 1) // (2 * ndevices)
    act = jax.nn.gelu(merger_input.astype(jnp.float32), approximate=False).astype(jnp.bfloat16)
    merged = jnp.dot(
        act,
        lax.all_gather(merger_weight, "dp", axis=0, tiled=True),
        preferred_element_type=jnp.float32,
    )
    merged = merged + merger_bias
    scale = lax.rsqrt(jnp.mean(merged * merged, axis=1, keepdims=True) + 1e-06)
    normed = (merged * scale * norm_gain).astype(jnp.bfloat16)
    onehot = (
        expert_ids[:, :, None] == jnp.arange(experts_all, dtype=jnp.int32)[None, None, :]
    ).astype(jnp.int32)
    flat_hot = onehot.reshape(rows * choose, experts_all)
    before = jnp.cumsum(flat_hot, axis=0) - flat_hot
    position = jnp.sum(before * flat_hot, axis=1)
    slot_flat = expert_ids.reshape(rows * choose) * capacity + position
    repeated = jnp.repeat(normed, choose, axis=0)
    outgoing = jnp.zeros((experts_all * capacity, width), jnp.bfloat16).at[slot_flat].set(repeated)
    outgoing = outgoing.reshape(experts_all, capacity, width)
    received = lax.all_to_all(outgoing, "dp", split_axis=0, concat_axis=0, tiled=True)
    served = run_experts(received, gate_weight, up_weight, down_weight, ndevices)
    returned = lax.all_to_all(served, "dp", split_axis=0, concat_axis=0, tiled=True)
    returned = returned.reshape(experts_all * capacity, width)
    picked = returned[slot_flat].reshape(rows, choose, width)
    counts = combine_ints.astype(jnp.float32)
    weights = counts / jnp.sum(counts, axis=1, keepdims=True)
    combined = jnp.sum(weights[:, :, None] * picked.astype(jnp.float32), axis=1)
    return (merged + combined).astype(jnp.bfloat16)


def swap_pairs(n):
    return [(i, i ^ 1) for i in range(n)]


def ring_order(chips):
    half = chips // 2
    return [2 * z for z in range(half)] + [2 * z + 1 for z in reversed(range(half))]


def ring_pairs(chips, by):
    order = ring_order(chips)
    pairs = []
    for spot, chip in enumerate(order):
        target = order[(spot + by) % chips]
        pairs += [(2 * chip, 2 * target), (2 * chip + 1, 2 * target + 1)]
    return pairs


def chip_at(chips, offset):
    chip = lax.axis_index(DP) // 2
    spot = jnp.where(chip % 2 == 0, chip // 2, chips - 1 - chip // 2)
    spot = lax.rem(spot + offset, chips)
    return jnp.where(spot < chips // 2, 2 * spot, 2 * (chips - 1 - spot) + 1)


def tile_of(extent, most):
    return max(t for t in range(LANES, most + 1, LANES) if extent % t == 0)


def kernel(body, outs, ins, scratch=(), limit=12 * MIB, flops=0, moved=0):
    return pl.pallas_call(
        body,
        out_shape=outs,
        in_specs=[VMEM] * len(ins),
        out_specs=jax.tree.map(lambda _: VMEM, outs),
        scratch_shapes=list(scratch),
        compiler_params=pltpu.CompilerParams(vmem_limit_bytes=limit),
        cost_estimate=pl.CostEstimate(flops=flops, bytes_accessed=moved, transcendentals=0),
    )(*ins)


def shaped(rows, width, dtype=jnp.bfloat16):
    return jax.ShapeDtypeStruct((rows, width), dtype)


def serve_body(blocks, *refs):
    ins = refs[:blocks]
    gate_ref, up_ref, down_ref, own_ref, other_ref, x_ref, h_ref = refs[blocks:]
    width, wide = gate_ref.shape
    expert = lax.axis_index(DP)
    start = 0
    share = []
    for ref in ins:
        size = ref.shape[0]
        x_ref[start : start + size, :] = ref[:, :width]
        tags = ref[:, width:].astype(jnp.float32)
        mine = lax.broadcasted_iota(jnp.int32, tags.shape, 1) == expert
        chosen = jnp.sum(jnp.where(mine, tags, 0.0), axis=1, keepdims=True)
        share.append(chosen / jnp.sum(tags, axis=1, keepdims=True))
        start += size
    share = jnp.concatenate(share, axis=0)
    tile = tile_of(wide, 256)
    for at in range(0, wide, tile):
        x = x_ref[...]
        gate = jnp.dot(x, gate_ref[:, at : at + tile], preferred_element_type=jnp.float32)
        up = jnp.dot(x, up_ref[:, at : at + tile], preferred_element_type=jnp.float32)
        h_ref[:, at : at + tile] = (gate * (1.0 / (1.0 + jnp.exp(-gate))) * up * share).astype(jnp.bfloat16)
    half = start // 2
    tile = tile_of(width, 512)
    for at in range(0, width, tile):
        out = jnp.dot(h_ref[...], down_ref[:, at : at + tile], preferred_element_type=jnp.float32)
        own_ref[:, at : at + tile] = out[:half].astype(jnp.bfloat16)
        other_ref[:, at : at + tile] = out[half:].astype(jnp.bfloat16)


def serve(ins, experts):
    rows = sum(x.shape[0] for x in ins)
    width, wide = experts[0].shape
    return kernel(
        functools.partial(serve_body, len(ins)),
        [shaped(rows // 2, width)] * 2,
        [*ins, *experts],
        [pltpu.VMEM((rows, width), jnp.bfloat16), pltpu.VMEM((rows, wide), jnp.bfloat16)],
        24 * MIB,
        6 * rows * width * wide,
        6 * width * wide,
    )


def tag_body(ids_ref, counts_ref, out_ref):
    rows, lanes = out_ref.shape
    expert = lax.broadcasted_iota(jnp.int32, (lanes, rows), 0)
    total = jnp.zeros((lanes, rows), jnp.float32)
    for k in range(ids_ref.shape[0]):
        total += jnp.where(expert == ids_ref[k : k + 1, :], counts_ref[k : k + 1, :].astype(jnp.float32), 0.0)
    out_ref[...] = total.T.astype(jnp.bfloat16)


def bulk_body(chips, offsets, act_ref, *refs):
    pieces, out_ref = refs[:-1], refs[-1]
    width = out_ref.shape[1]
    tile = tile_of(width, 512)
    for at in range(0, width, tile):
        total = None
        for offset, piece in zip(offsets, pieces):
            act = act_ref[chip_at(chips, offset)]
            part = jnp.dot(act, piece[:, at : at + tile], preferred_element_type=jnp.float32)
            total = part if total is None else total + part
        out_ref[:, at : at + tile] = total


def last_body(chips, act_ref, total_ref, top_ref, bottom_ref, *outs):
    width = total_ref.shape[1]
    mid = top_ref.shape[0]
    rows = outs[0].shape[0]
    tile = tile_of(width, 512)
    act = act_ref[chip_at(chips, chips // 2)]
    for at in range(0, width, tile):
        to = at + tile
        total = total_ref[:, at:to]
        total += jnp.dot(act[:, :mid], top_ref[:, at:to], preferred_element_type=jnp.float32)
        total += jnp.dot(act[:, mid:], bottom_ref[:, at:to], preferred_element_type=jnp.float32)
        for index, out in enumerate(outs):
            out[:, at:to] = total[index * rows : (index + 1) * rows]


def norm_body(parts, *refs):
    bias_ref, gain_ref, tags_ref, merged_ref, low_ref, high_ref = refs[3 * parts :]
    width = merged_ref.shape[1]
    cut = low_ref.shape[0]
    low_ref[:, width:] = tags_ref[:cut, :]
    high_ref[:, width:] = tags_ref[cut:, :]
    at = 0
    square = 0.0
    for index in range(parts):
        own_ref, other_ref, cross_ref = refs[3 * index : 3 * index + 3]
        to = at + own_ref.shape[1]
        merged = own_ref[...] + other_ref[...] + bias_ref[:, at:to] + cross_ref[...].astype(jnp.float32)
        merged_ref[:, at:to] = merged
        square += jnp.sum(merged * merged, axis=1, keepdims=True)
        at = to
    scale = lax.rsqrt(square / width + 1e-06)
    low_ref[:, :width] = (merged_ref[:cut, :] * scale[:cut] * gain_ref[...]).astype(jnp.bfloat16)
    high_ref[:, :width] = (merged_ref[cut:, :] * scale[cut:] * gain_ref[...]).astype(jnp.bfloat16)


def plus_body(*refs):
    refs[-1][...] = (refs[0][...] + refs[1][...]).astype(refs[-1].dtype)


def add_body(at, shift, own_ref, other_ref, *refs):
    out_ref = refs[-1]
    size = out_ref.shape[0]
    total = own_ref[at : at + size, :].astype(jnp.float32) + other_ref[at : at + size, :].astype(jnp.float32)
    if len(refs) == 1:
        out_ref[...] = total.astype(jnp.bfloat16)
        return
    to = shift + refs[0].shape[0]
    out_ref[shift:to, :] = (total[shift:to] + refs[0][...].astype(jnp.float32)).astype(jnp.bfloat16)
    if shift > 0:
        out_ref[:shift, :] = total[:shift].astype(jnp.bfloat16)
    if to < size:
        out_ref[to:, :] = total[to:].astype(jnp.bfloat16)


def add(own, other, at, size, total=None, shift=0):
    ins = [own, other] + ([] if total is None else [total])
    return kernel(functools.partial(add_body, at, shift), shaped(size, own.shape[1]), ins)


def finish_body(merged_ref, *refs):
    out_ref = refs[-1]
    at = 0
    for index in range(0, len(refs) - 1, 4):
        ins = refs[index : index + 4]
        to = at + ins[0].shape[0]
        total = sum(ref[...].astype(jnp.float32) for ref in ins)
        out_ref[at:to, :] = (merged_ref[at:to, :] + total).astype(jnp.bfloat16)
        at = to


def dense(
    merger_input,
    merger_weight,
    merger_bias,
    norm_gain,
    gate_weight,
    up_weight,
    down_weight,
    expert_ids,
    combine_ints,
):
    n = lax.axis_size(DP)
    chips = n // 2
    far = chips // 2
    rows = merger_input.shape[0]
    depth, width = merger_weight.shape
    half = depth // 2
    cut = rows // 2
    first_core = lax.axis_index(DP) % 2 == 0
    first_group = lax.axis_index(GROUPS) == 0

    swap = functools.partial(lax.ppermute, axis_name=DP, perm=swap_pairs(n))
    cross = functools.partial(lax.ppermute, axis_name=GROUPS, perm=swap_pairs(2))
    rings = [functools.partial(lax.ppermute, axis_name=DP, perm=ring_pairs(chips, by)) for by in (1, -1)]

    def hop(way, array):
        return rings[way](array)

    zero = jnp.uint32(0)
    weight = lax.dynamic_slice(merger_weight, (lax.axis_index(GROUPS).astype(jnp.uint32) * half, zero), (half, width))
    act = jax.nn.gelu(merger_input.astype(jnp.float32), approximate=False).astype(jnp.bfloat16)
    act = act.reshape(rows, chips, 2, 2, half)
    kept = jnp.where(first_core, act[:, :, 0], act[:, :, 1])
    given = jnp.where(first_core, act[:, :, 1], act[:, :, 0])
    given = swap(given)
    act = jnp.concatenate([kept, given], axis=0)
    kept = jnp.where(first_group, act[:, :, 0], act[:, :, 1])
    given = jnp.where(first_group, act[:, :, 1], act[:, :, 0])
    given = cross(given)
    act = jnp.concatenate([kept, given], axis=0).transpose(1, 0, 2)

    lanes = -(-n // LANES) * LANES
    tags = kernel(tag_body, shaped(rows, lanes), [expert_ids.T, combine_ints.T])

    mid = (half + 15) // 16 * 8
    share = width // PARTS
    streams = []
    for part in range(PARTS):
        left = right = weight[:, part * share : (part + 1) * share]
        offsets, pieces = [0], [left]
        for step in range(1, far):
            left, right = hop(0, left), hop(1, right)
            offsets += [chips - step, step]
            pieces += [left, right]
        top, bottom = hop(0, left[:mid]), hop(1, right[mid:])
        size = 4 * rows * share
        total = kernel(
            functools.partial(bulk_body, chips, offsets),
            shaped(4 * rows, share, jnp.float32),
            [act, *pieces],
            flops=2 * size * half * chips,
            moved=4 * size,
        )
        own, own_other, theirs, theirs_other = kernel(
            functools.partial(last_body, chips),
            [shaped(rows, share, jnp.float32)] * 4,
            [act, total, top, bottom],
            flops=2 * size * half,
            moved=8 * size,
        )
        theirs_other = swap(theirs_other)
        theirs = kernel(plus_body, shaped(rows, share), [theirs, theirs_other])
        theirs = cross(theirs)
        streams += [own, swap(own_other), theirs]
    merged, *block = kernel(
        functools.partial(norm_body, PARTS),
        [shaped(rows, width, jnp.float32)] + [shaped(cut, width + lanes)] * 2,
        [*streams, merger_bias[None], norm_gain[None], tags],
    )

    experts = [w[0] for w in (gate_weight, up_weight, down_weight)]
    arrived = [[(own,) for own in block]]
    sides = [(own, own) for own in block]
    for _ in range(1, far):
        sides = [tuple(hop(way, side[way]) for way in (0, 1)) for side in sides]
        arrived.append(sides)
    short = cut // 2
    arrived.append([(hop(0, side[0][:short]), hop(1, side[1][short:])) for side in sides])

    def served(ins):
        others = [swap(x) for x in ins]
        own, other = serve([*ins, *others], experts)
        return own, swap(other)

    outs = [[served(ins) for ins in pair] for pair in arrived]

    def home(way, which):
        total = add(*outs[far][which], way * short, short)
        total = hop(way, total)
        for step in reversed(range(1, far)):
            total = add(*outs[step][which], (1 - way) * cut, cut, total, way * short if step == far - 1 else 0)
            total = hop(way, total)
        return total

    sums = [(*outs[0][which], home(0, which), home(1, which)) for which in (0, 1)]
    return kernel(finish_body, shaped(rows, width), [merged, *sums[0], *sums[1]])


def shards(*arrays):
    gate_weight, expert_ids = arrays[4], arrays[7]
    n = lax.axis_size(DP)
    rows, choose = expert_ids.shape
    capacity = (3 * rows * choose + 2 * n - 1) // (2 * n)
    if lax.axis_size(GROUPS) == 2 and gate_weight.shape[0] == 1 and n % 4 == 0 and n >= 16 and 2 * capacity >= rows:
        return dense(*arrays)
    return routed(*arrays)


def solution(mesh):
    placed = (
        P(("groups", "dp"), None),
        P("dp", None),
        P(),
        P(),
        P("dp", None, None),
        P("dp", None, None),
        P("dp", None, None),
        P(("groups", "dp"), None),
        P(("groups", "dp"), None),
    )
    return jax.shard_map(
        shards, mesh=mesh, in_specs=placed, out_specs=P(("groups", "dp"), None), check_vma=False
    )
```

```python
import functools

import jax
import jax.numpy as jnp
from jax import lax
from jax.experimental import pallas as pl
from jax.experimental.pallas import tpu as pltpu
from jax.sharding import PartitionSpec as P


LANES = 128
MIB = 1024 * 1024
PARTS = 2
DP = "dp"
GROUPS = "groups"
VMEM = pl.BlockSpec(memory_space=pltpu.VMEM)


def run_experts(received, gate_weight, up_weight, down_weight, ndevices):
    local = gate_weight.shape[0]
    slots = received.shape[1]
    width = received.shape[2]
    inputs = received.reshape(ndevices, local, slots, width)
    gate = jnp.einsum("jlcd,ldh->jlch", inputs, gate_weight, preferred_element_type=jnp.float32)
    up = jnp.einsum("jlcd,ldh->jlch", inputs, up_weight, preferred_element_type=jnp.float32)
    hidden = (jax.nn.silu(gate) * up).astype(jnp.bfloat16)
    output = jnp.einsum("jlch,lhd->jlcd", hidden, down_weight, preferred_element_type=jnp.float32)
    return output.astype(jnp.bfloat16).reshape(ndevices * local, slots, width)


def routed(
    merger_input,
    merger_weight,
    merger_bias,
    norm_gain,
    gate_weight,
    up_weight,
    down_weight,
    expert_ids,
    combine_ints,
):
    ndevices = lax.axis_size("dp")
    rows = merger_input.shape[0]
    width = merger_weight.shape[1]
    choose = expert_ids.shape[1]
    experts_all = gate_weight.shape[0] * ndevices
    capacity = (3 * rows * choose + 2 * ndevices - 1) // (2 * ndevices)
    act = jax.nn.gelu(merger_input.astype(jnp.float32), approximate=False).astype(jnp.bfloat16)
    merged = jnp.dot(
        act,
        lax.all_gather(merger_weight, "dp", axis=0, tiled=True),
        preferred_element_type=jnp.float32,
    )
    merged = merged + merger_bias
    scale = lax.rsqrt(jnp.mean(merged * merged, axis=1, keepdims=True) + 1e-06)
    normed = (merged * scale * norm_gain).astype(jnp.bfloat16)
    onehot = (
        expert_ids[:, :, None] == jnp.arange(experts_all, dtype=jnp.int32)[None, None, :]
    ).astype(jnp.int32)
    flat_hot = onehot.reshape(rows * choose, experts_all)
    before = jnp.cumsum(flat_hot, axis=0) - flat_hot
    position = jnp.sum(before * flat_hot, axis=1)
    slot_flat = expert_ids.reshape(rows * choose) * capacity + position
    repeated = jnp.repeat(normed, choose, axis=0)
    outgoing = jnp.zeros((experts_all * capacity, width), jnp.bfloat16).at[slot_flat].set(repeated)
    outgoing = outgoing.reshape(experts_all, capacity, width)
    received = lax.all_to_all(outgoing, "dp", split_axis=0, concat_axis=0, tiled=True)
    served = run_experts(received, gate_weight, up_weight, down_weight, ndevices)
    returned = lax.all_to_all(served, "dp", split_axis=0, concat_axis=0, tiled=True)
    returned = returned.reshape(experts_all * capacity, width)
    picked = returned[slot_flat].reshape(rows, choose, width)
    counts = combine_ints.astype(jnp.float32)
    weights = counts / jnp.sum(counts, axis=1, keepdims=True)
    combined = jnp.sum(weights[:, :, None] * picked.astype(jnp.float32), axis=1)
    return (merged + combined).astype(jnp.bfloat16)


def swap_pairs(n):
    return [(i, i ^ 1) for i in range(n)]


def ring_order(chips):
    half = chips // 2
    return [2 * z for z in range(half)] + [2 * z + 1 for z in reversed(range(half))]


def ring_pairs(chips, by):
    order = ring_order(chips)
    pairs = []
    for spot, chip in enumerate(order):
        target = order[(spot + by) % chips]
        pairs += [(2 * chip, 2 * target), (2 * chip + 1, 2 * target + 1)]
    return pairs


def chip_at(chips, offset):
    chip = lax.axis_index(DP) // 2
    spot = jnp.where(chip % 2 == 0, chip // 2, chips - 1 - chip // 2)
    spot = lax.rem(spot + offset, chips)
    return jnp.where(spot < chips // 2, 2 * spot, 2 * (chips - 1 - spot) + 1)


def tile_of(extent, most):
    return max(t for t in range(LANES, most + 1, LANES) if extent % t == 0)


def kernel(body, outs, ins, scratch=(), limit=12 * MIB, flops=0, moved=0):
    return pl.pallas_call(
        body,
        out_shape=outs,
        in_specs=[VMEM] * len(ins),
        out_specs=jax.tree.map(lambda _: VMEM, outs),
        scratch_shapes=list(scratch),
        compiler_params=pltpu.CompilerParams(vmem_limit_bytes=limit),
        cost_estimate=pl.CostEstimate(flops=flops, bytes_accessed=moved, transcendentals=0),
    )(*ins)


def shaped(rows, width, dtype=jnp.bfloat16):
    return jax.ShapeDtypeStruct((rows, width), dtype)


def serve_body(blocks, which, experts, *refs):
    ins, tagged = refs[:blocks], refs[: blocks * (which + 1)][-blocks:]
    gate_ref, up_ref, down_ref, own_ref, other_ref, x_ref, h_ref = refs[blocks * (which + 1) :]
    width, wide = gate_ref.shape
    start = 0
    share = []
    for ref, tag in zip(ins, tagged):
        size = ref.shape[0]
        x_ref[start : start + size, :] = ref[:, :width]
        tags = tag[:, width:].astype(jnp.float32)
        lane = lax.broadcasted_iota(jnp.int32, tags.shape, 1) - which * experts
        chosen = jnp.sum(jnp.where(lane == lax.axis_index(DP), tags, 0.0), axis=1, keepdims=True)
        whole = jnp.sum(jnp.where((lane >= 0) & (lane < experts), tags, 0.0), axis=1, keepdims=True)
        share.append(chosen / whole)
        start += size
    share = jnp.concatenate(share, axis=0)
    tile = tile_of(wide, 256)
    for at in range(0, wide, tile):
        x = x_ref[...]
        gate = jnp.dot(x, gate_ref[:, at : at + tile], preferred_element_type=jnp.float32)
        up = jnp.dot(x, up_ref[:, at : at + tile], preferred_element_type=jnp.float32)
        h_ref[:, at : at + tile] = (gate * (1.0 / (1.0 + jnp.exp(-gate))) * up * share).astype(jnp.bfloat16)
    half = start // 2
    tile = tile_of(width, 512)
    for at in range(0, width, tile):
        out = jnp.dot(h_ref[...], down_ref[:, at : at + tile], preferred_element_type=jnp.float32)
        own_ref[:, at : at + tile] = out[:half].astype(jnp.bfloat16)
        other_ref[:, at : at + tile] = out[half:].astype(jnp.bfloat16)


def serve(which, ins, tagged, weights):
    rows = sum(x.shape[0] for x in ins)
    width, wide = weights[0].shape
    return kernel(
        functools.partial(serve_body, len(ins), which, lax.axis_size(DP)),
        [shaped(rows // 2, width)] * 2,
        [*ins, *tagged, *weights],
        [pltpu.VMEM((rows, width), jnp.bfloat16), pltpu.VMEM((rows, wide), jnp.bfloat16)],
        24 * MIB,
        6 * rows * width * wide,
        6 * width * wide,
    )


def tag_body(experts, ids_ref, counts_ref, out_ref):
    cut, lanes = out_ref.shape
    lane = lax.broadcasted_iota(jnp.int32, (lanes, ids_ref.shape[1]), 0)
    total = jnp.zeros(lane.shape, jnp.float32)
    for k in range(ids_ref.shape[0]):
        counts = counts_ref[k : k + 1, :].astype(jnp.float32)
        total += jnp.where(lane % experts == ids_ref[k : k + 1, :], counts, 0.0)
    total = total.T
    lane = lax.broadcasted_iota(jnp.int32, (cut, lanes), 1)
    total = jnp.where(lane < experts, total[:cut], jnp.where(lane < 2 * experts, total[cut:], 0.0))
    out_ref[...] = total.astype(jnp.bfloat16)


def bulk_body(chips, offsets, act_ref, *refs):
    pieces, out_ref = refs[:-1], refs[-1]
    width = out_ref.shape[1]
    tile = tile_of(width, 512)
    for at in range(0, width, tile):
        total = None
        for offset, piece in zip(offsets, pieces):
            act = act_ref[chip_at(chips, offset)]
            part = jnp.dot(act, piece[:, at : at + tile], preferred_element_type=jnp.float32)
            total = part if total is None else total + part
        out_ref[:, at : at + tile] = total


def last_body(chips, act_ref, total_ref, top_ref, bottom_ref, *outs):
    width = total_ref.shape[1]
    mid = top_ref.shape[0]
    rows = outs[0].shape[0]
    tile = tile_of(width, 512)
    act = act_ref[chip_at(chips, chips // 2)]
    for at in range(0, width, tile):
        to = at + tile
        total = total_ref[:, at:to]
        total += jnp.dot(act[:, :mid], top_ref[:, at:to], preferred_element_type=jnp.float32)
        total += jnp.dot(act[:, mid:], bottom_ref[:, at:to], preferred_element_type=jnp.float32)
        for index, out in enumerate(outs):
            out[:, at:to] = total[index * rows : (index + 1) * rows]


def norm_body(parts, *refs):
    bias_ref, gain_ref, tags_ref, merged_ref, low_ref, high_ref = refs[3 * parts :]
    width = merged_ref.shape[1]
    cut = low_ref.shape[0]
    low_ref[:, width:] = tags_ref[...]
    at = 0
    square = 0.0
    for index in range(parts):
        own_ref, other_ref, cross_ref = refs[3 * index : 3 * index + 3]
        to = at + own_ref.shape[1]
        merged = own_ref[...] + other_ref[...] + bias_ref[:, at:to] + cross_ref[...].astype(jnp.float32)
        merged_ref[:, at:to] = merged
        square += jnp.sum(merged * merged, axis=1, keepdims=True)
        at = to
    scale = lax.rsqrt(square / width + 1e-06)
    low_ref[:, :width] = (merged_ref[:cut, :] * scale[:cut] * gain_ref[...]).astype(jnp.bfloat16)
    high_ref[...] = (merged_ref[cut:, :] * scale[cut:] * gain_ref[...]).astype(jnp.bfloat16)


def plus_body(*refs):
    refs[-1][...] = (refs[0][...] + refs[1][...]).astype(refs[-1].dtype)


def add_body(at, shift, own_ref, other_ref, *refs):
    out_ref = refs[-1]
    size = out_ref.shape[0]
    total = own_ref[at : at + size, :].astype(jnp.float32) + other_ref[at : at + size, :].astype(jnp.float32)
    if len(refs) == 1:
        out_ref[...] = total.astype(jnp.bfloat16)
        return
    to = shift + refs[0].shape[0]
    out_ref[shift:to, :] = (total[shift:to] + refs[0][...].astype(jnp.float32)).astype(jnp.bfloat16)
    if shift > 0:
        out_ref[:shift, :] = total[:shift].astype(jnp.bfloat16)
    if to < size:
        out_ref[to:, :] = total[to:].astype(jnp.bfloat16)


def add(own, other, at, size, total=None, shift=0):
    ins = [own, other] + ([] if total is None else [total])
    return kernel(functools.partial(add_body, at, shift), shaped(size, own.shape[1]), ins)


def finish_body(merged_ref, *refs):
    out_ref = refs[-1]
    at = 0
    for index in range(0, len(refs) - 1, 4):
        ins = refs[index : index + 4]
        to = at + ins[0].shape[0]
        total = sum(ref[...].astype(jnp.float32) for ref in ins)
        out_ref[at:to, :] = (merged_ref[at:to, :] + total).astype(jnp.bfloat16)
        at = to


def dense(
    merger_input,
    merger_weight,
    merger_bias,
    norm_gain,
    gate_weight,
    up_weight,
    down_weight,
    expert_ids,
    combine_ints,
):
    n = lax.axis_size(DP)
    chips = n // 2
    far = chips // 2
    rows = merger_input.shape[0]
    depth, width = merger_weight.shape
    half = depth // 2
    cut = rows // 2
    first_core = lax.axis_index(DP) % 2 == 0
    first_group = lax.axis_index(GROUPS) == 0

    swap = functools.partial(lax.ppermute, axis_name=DP, perm=swap_pairs(n))
    cross = functools.partial(lax.ppermute, axis_name=GROUPS, perm=swap_pairs(2))
    rings = [functools.partial(lax.ppermute, axis_name=DP, perm=ring_pairs(chips, by)) for by in (1, -1)]

    def hop(way, array):
        return rings[way](array)

    first = lax.axis_index(GROUPS).astype(jnp.uint32) * half
    act = jax.nn.gelu(merger_input.astype(jnp.float32), approximate=False).astype(jnp.bfloat16)
    act = act.reshape(rows, chips, 2, 2, half)
    kept = jnp.where(first_core, act[:, :, 0], act[:, :, 1])
    given = jnp.where(first_core, act[:, :, 1], act[:, :, 0])
    given = swap(given)
    act = jnp.concatenate([kept, given], axis=0)
    kept = jnp.where(first_group, act[:, :, 0], act[:, :, 1])
    given = jnp.where(first_group, act[:, :, 1], act[:, :, 0])
    given = cross(given)
    act = jnp.concatenate([kept, given], axis=0).transpose(1, 0, 2)

    lanes = -(-2 * n // LANES) * LANES
    tags = kernel(functools.partial(tag_body, n), shaped(cut, lanes), [expert_ids.T, combine_ints.T])

    mid = (half + 15) // 16 * 8
    share = width // PARTS
    streams = []
    for part in range(PARTS):
        weight = merger_weight if part == 0 else lax.optimization_barrier(merger_weight)
        left = right = lax.dynamic_slice(weight, (first, jnp.uint32(part * share)), (half, share))
        offsets, pieces = [0], [left]
        for step in range(1, far):
            left, right = hop(0, left), hop(1, right)
            offsets += [chips - step, step]
            pieces += [left, right]
        top, bottom = hop(0, left[:mid]), hop(1, right[mid:])
        size = 4 * rows * share
        total = kernel(
            functools.partial(bulk_body, chips, offsets),
            shaped(4 * rows, share, jnp.float32),
            [act, *pieces],
            flops=2 * size * half * chips,
            moved=4 * size,
        )
        own, own_other, theirs, theirs_other = kernel(
            functools.partial(last_body, chips),
            [shaped(rows, share, jnp.float32)] * 4,
            [act, total, top, bottom],
            flops=2 * size * half,
            moved=8 * size,
        )
        theirs_other = swap(theirs_other)
        theirs = kernel(plus_body, shaped(rows, share), [theirs, theirs_other])
        theirs = cross(theirs)
        streams += [own, swap(own_other), theirs]
    merged, *block = kernel(
        functools.partial(norm_body, PARTS),
        [shaped(rows, width, jnp.float32), shaped(cut, width + lanes), shaped(cut, width)],
        [*streams, merger_bias[None], norm_gain[None], tags],
    )

    experts = [w[0] for w in (gate_weight, up_weight, down_weight)]
    arrived = [[(own,) for own in block]]
    sides = [(own, own) for own in block]
    for _ in range(1, far):
        sides = [tuple(hop(way, side[way]) for way in (0, 1)) for side in sides]
        arrived.append(sides)
    short = cut // 2
    arrived.append([(hop(0, side[0][:short]), hop(1, side[1][short:])) for side in sides])

    outs = []
    for step, pair in enumerate(arrived):
        tagged = []
        outs.append([])
        for which, ins in enumerate(pair):
            ins = [*ins, *(swap(x) for x in ins)]
            own, other = serve(which, ins, tagged, experts)
            tagged = ins
            outs[step].append((own, swap(other)))

    def home(way, which):
        total = add(*outs[far][which], way * short, short)
        total = hop(way, total)
        for step in reversed(range(1, far)):
            total = add(*outs[step][which], (1 - way) * cut, cut, total, way * short if step == far - 1 else 0)
            total = hop(way, total)
        return total

    sums = [(*outs[0][which], home(0, which), home(1, which)) for which in (0, 1)]
    return kernel(finish_body, shaped(rows, width), [merged, *sums[0], *sums[1]])


def shards(*arrays):
    gate_weight, expert_ids = arrays[4], arrays[7]
    n = lax.axis_size(DP)
    rows, choose = expert_ids.shape
    capacity = (3 * rows * choose + 2 * n - 1) // (2 * n)
    if lax.axis_size(GROUPS) == 2 and gate_weight.shape[0] == 1 and n % 4 == 0 and n >= 16 and 2 * capacity >= rows:
        return dense(*arrays)
    return routed(*arrays)


def solution(mesh):
    placed = (
        P(("groups", "dp"), None),
        P("dp", None),
        P(),
        P(),
        P("dp", None, None),
        P("dp", None, None),
        P("dp", None, None),
        P(("groups", "dp"), None),
        P(("groups", "dp"), None),
    )
    return jax.shard_map(
        shards, mesh=mesh, in_specs=placed, out_specs=P(("groups", "dp"), None), check_vma=False
    )
```

```python
import functools
import math

import jax
import jax.numpy as jnp
import numpy as np
from jax import lax
from jax.experimental import pallas as pl
from jax.experimental.pallas import tpu as pltpu
from jax.sharding import PartitionSpec as P


LANES = 128
MIB = 1024 * 1024
PARTS = 2
DP = "dp"
GROUPS = "groups"
VMEM = pl.BlockSpec(memory_space=pltpu.VMEM)


def run_experts(received, gate_weight, up_weight, down_weight, ndevices):
    local = gate_weight.shape[0]
    slots = received.shape[1]
    width = received.shape[2]
    inputs = received.reshape(ndevices, local, slots, width)
    gate = jnp.einsum("jlcd,ldh->jlch", inputs, gate_weight, preferred_element_type=jnp.float32)
    up = jnp.einsum("jlcd,ldh->jlch", inputs, up_weight, preferred_element_type=jnp.float32)
    hidden = (jax.nn.silu(gate) * up).astype(jnp.bfloat16)
    output = jnp.einsum("jlch,lhd->jlcd", hidden, down_weight, preferred_element_type=jnp.float32)
    return output.astype(jnp.bfloat16).reshape(ndevices * local, slots, width)


def routed(
    merger_input,
    merger_weight,
    merger_bias,
    norm_gain,
    gate_weight,
    up_weight,
    down_weight,
    expert_ids,
    combine_ints,
):
    ndevices = lax.axis_size("dp")
    rows = merger_input.shape[0]
    width = merger_weight.shape[1]
    choose = expert_ids.shape[1]
    experts_all = gate_weight.shape[0] * ndevices
    capacity = (3 * rows * choose + 2 * ndevices - 1) // (2 * ndevices)
    act = jax.nn.gelu(merger_input.astype(jnp.float32), approximate=False).astype(jnp.bfloat16)
    merged = jnp.dot(
        act,
        lax.all_gather(merger_weight, "dp", axis=0, tiled=True),
        preferred_element_type=jnp.float32,
    )
    merged = merged + merger_bias
    scale = lax.rsqrt(jnp.mean(merged * merged, axis=1, keepdims=True) + 1e-06)
    normed = (merged * scale * norm_gain).astype(jnp.bfloat16)
    onehot = (
        expert_ids[:, :, None] == jnp.arange(experts_all, dtype=jnp.int32)[None, None, :]
    ).astype(jnp.int32)
    flat_hot = onehot.reshape(rows * choose, experts_all)
    before = jnp.cumsum(flat_hot, axis=0) - flat_hot
    position = jnp.sum(before * flat_hot, axis=1)
    slot_flat = expert_ids.reshape(rows * choose) * capacity + position
    repeated = jnp.repeat(normed, choose, axis=0)
    outgoing = jnp.zeros((experts_all * capacity, width), jnp.bfloat16).at[slot_flat].set(repeated)
    outgoing = outgoing.reshape(experts_all, capacity, width)
    received = lax.all_to_all(outgoing, "dp", split_axis=0, concat_axis=0, tiled=True)
    served = run_experts(received, gate_weight, up_weight, down_weight, ndevices)
    returned = lax.all_to_all(served, "dp", split_axis=0, concat_axis=0, tiled=True)
    returned = returned.reshape(experts_all * capacity, width)
    picked = returned[slot_flat].reshape(rows, choose, width)
    counts = combine_ints.astype(jnp.float32)
    weights = counts / jnp.sum(counts, axis=1, keepdims=True)
    combined = jnp.sum(weights[:, :, None] * picked.astype(jnp.float32), axis=1)
    return (merged + combined).astype(jnp.bfloat16)


def swap_pairs(n):
    return [(i, i ^ 1) for i in range(n)]


def ring_order(chips):
    half = chips // 2
    return [2 * z for z in range(half)] + [2 * z + 1 for z in reversed(range(half))]


def ring_pairs(chips, by):
    order = ring_order(chips)
    pairs = []
    for spot, chip in enumerate(order):
        target = order[(spot + by) % chips]
        pairs += [(2 * chip, 2 * target), (2 * chip + 1, 2 * target + 1)]
    return pairs


def chip_at(chips, offset):
    chip = lax.axis_index(DP) // 2
    spot = jnp.where(chip % 2 == 0, chip // 2, chips - 1 - chip // 2)
    spot = lax.rem(spot + offset, chips)
    return jnp.where(spot < chips // 2, 2 * spot, 2 * (chips - 1 - spot) + 1)


def tile_of(extent, most):
    return max(t for t in range(LANES, most + 1, LANES) if extent % t == 0)


def kernel(body, outs, ins, scratch=(), limit=12 * MIB, flops=0, moved=0):
    return pl.pallas_call(
        body,
        out_shape=outs,
        in_specs=[VMEM] * len(ins),
        out_specs=jax.tree.map(lambda _: VMEM, outs),
        scratch_shapes=list(scratch),
        compiler_params=pltpu.CompilerParams(vmem_limit_bytes=limit),
        cost_estimate=pl.CostEstimate(flops=flops, bytes_accessed=moved, transcendentals=0),
    )(*ins)


def shaped(rows, width, dtype=jnp.bfloat16):
    return jax.ShapeDtypeStruct((rows, width), dtype)


def serve_body(blocks, which, experts, *refs):
    ins, tagged = refs[:blocks], refs[: blocks * (which + 1)][-blocks:]
    gate_ref, up_ref, down_ref, own_ref, other_ref, x_ref, h_ref = refs[blocks * (which + 1) :]
    width, wide = gate_ref.shape
    start = 0
    share = []
    for ref, tag in zip(ins, tagged):
        size = ref.shape[0]
        x_ref[start : start + size, :] = ref[:, :width]
        tags = tag[:, width:].astype(jnp.float32)
        lane = lax.broadcasted_iota(jnp.int32, tags.shape, 1) - which * experts
        chosen = jnp.sum(jnp.where(lane == lax.axis_index(DP), tags, 0.0), axis=1, keepdims=True)
        whole = jnp.sum(jnp.where((lane >= 0) & (lane < experts), tags, 0.0), axis=1, keepdims=True)
        share.append(chosen / whole)
        start += size
    share = jnp.concatenate(share, axis=0)
    tile = tile_of(wide, 256)
    for at in range(0, wide, tile):
        x = x_ref[...]
        gate = jnp.dot(x, gate_ref[:, at : at + tile], preferred_element_type=jnp.float32)
        up = jnp.dot(x, up_ref[:, at : at + tile], preferred_element_type=jnp.float32)
        h_ref[:, at : at + tile] = (gate * (1.0 / (1.0 + jnp.exp(-gate))) * up * share).astype(jnp.bfloat16)
    half = start // 2
    tile = tile_of(width, 512)
    for at in range(0, width, tile):
        out = jnp.dot(h_ref[...], down_ref[:, at : at + tile], preferred_element_type=jnp.float32)
        own_ref[:, at : at + tile] = out[:half].astype(jnp.bfloat16)
        other_ref[:, at : at + tile] = out[half:].astype(jnp.bfloat16)


def serve(which, ins, tagged, weights):
    rows = sum(x.shape[0] for x in ins)
    width, wide = weights[0].shape
    return kernel(
        functools.partial(serve_body, len(ins), which, lax.axis_size(DP)),
        [shaped(rows // 2, width)] * 2,
        [*ins, *tagged, *weights],
        [pltpu.VMEM((rows, width), jnp.bfloat16), pltpu.VMEM((rows, wide), jnp.bfloat16)],
        24 * MIB,
        6 * rows * width * wide,
        6 * width * wide,
    )


def tag_body(experts, ids_ref, counts_ref, out_ref):
    cut, lanes = out_ref.shape
    lane = lax.broadcasted_iota(jnp.int32, (lanes, ids_ref.shape[1]), 0)
    total = jnp.zeros(lane.shape, jnp.float32)
    for k in range(ids_ref.shape[0]):
        counts = counts_ref[k : k + 1, :].astype(jnp.float32)
        total += jnp.where(lane % experts == ids_ref[k : k + 1, :], counts, 0.0)
    total = total.T
    lane = lax.broadcasted_iota(jnp.int32, (cut, lanes), 1)
    total = jnp.where(lane < experts, total[:cut], jnp.where(lane < 2 * experts, total[cut:], 0.0))
    out_ref[...] = total.astype(jnp.bfloat16)


def gelu_body(chips, in_ref, mine_ref, given_ref):
    half = mine_ref.shape[3]
    first_core = lax.axis_index(DP) % 2 == 0
    first_group = lax.axis_index(GROUPS) == 0
    for chip in range(chips):
        x = in_ref[:, chip * 4 * half : (chip + 1) * 4 * half].astype(jnp.float32)
        act = 0.5 * x * (1.0 + lax.erf(x * np.float32(math.sqrt(0.5))))
        cuts = [act[:, at * half : (at + 1) * half] for at in range(4)]
        for ref, near, away in ((mine_ref, 0, 2), (given_ref, 2, 0)):
            low = jnp.where(first_core, cuts[near], cuts[away])
            high = jnp.where(first_core, cuts[near + 1], cuts[away + 1])
            ref[0, chip] = jnp.where(first_group, low, high).astype(jnp.bfloat16)
            ref[1, chip] = jnp.where(first_group, high, low).astype(jnp.bfloat16)


def rows_of(refs, chip):
    mine_ref, given_ref, theirs_ref = refs
    return jnp.concatenate([mine_ref[0, chip], given_ref[0, chip], theirs_ref[0, chip], theirs_ref[1, chip]], axis=0)


def bulk_body(chips, offsets, *refs):
    pieces, out_ref = refs[3:-1], refs[-1]
    width = out_ref.shape[1]
    tile = tile_of(width, 512)
    for at in range(0, width, tile):
        total = None
        for offset, piece in zip(offsets, pieces):
            act = rows_of(refs[:3], chip_at(chips, offset))
            part = jnp.dot(act, piece[:, at : at + tile], preferred_element_type=jnp.float32)
            total = part if total is None else total + part
        out_ref[:, at : at + tile] = total


def last_body(chips, mine_ref, given_ref, theirs_ref, total_ref, top_ref, bottom_ref, *outs):
    width = total_ref.shape[1]
    mid = top_ref.shape[0]
    rows = outs[0].shape[0]
    tile = tile_of(width, 512)
    act = rows_of((mine_ref, given_ref, theirs_ref), chip_at(chips, chips // 2))
    for at in range(0, width, tile):
        to = at + tile
        total = total_ref[:, at:to]
        total += jnp.dot(act[:, :mid], top_ref[:, at:to], preferred_element_type=jnp.float32)
        total += jnp.dot(act[:, mid:], bottom_ref[:, at:to], preferred_element_type=jnp.float32)
        for index, out in enumerate(outs):
            out[:, at:to] = total[index * rows : (index + 1) * rows]


def norm_body(parts, *refs):
    bias_ref, gain_ref, tags_ref, merged_ref, low_ref, high_ref = refs[3 * parts :]
    width = merged_ref.shape[1]
    cut = low_ref.shape[0]
    low_ref[:, width:] = tags_ref[...]
    at = 0
    square = 0.0
    for index in range(parts):
        own_ref, other_ref, cross_ref = refs[3 * index : 3 * index + 3]
        to = at + own_ref.shape[1]
        merged = own_ref[...] + other_ref[...] + bias_ref[:, at:to] + cross_ref[...].astype(jnp.float32)
        merged_ref[:, at:to] = merged
        square += jnp.sum(merged * merged, axis=1, keepdims=True)
        at = to
    scale = lax.rsqrt(square / width + 1e-06)
    low_ref[:, :width] = (merged_ref[:cut, :] * scale[:cut] * gain_ref[...]).astype(jnp.bfloat16)
    high_ref[...] = (merged_ref[cut:, :] * scale[cut:] * gain_ref[...]).astype(jnp.bfloat16)


def plus_body(*refs):
    refs[-1][...] = (refs[0][...] + refs[1][...]).astype(refs[-1].dtype)


def add_body(at, shift, own_ref, other_ref, *refs):
    out_ref = refs[-1]
    size = out_ref.shape[0]
    total = own_ref[at : at + size, :].astype(jnp.float32) + other_ref[at : at + size, :].astype(jnp.float32)
    if len(refs) == 1:
        out_ref[...] = total.astype(jnp.bfloat16)
        return
    to = shift + refs[0].shape[0]
    out_ref[shift:to, :] = (total[shift:to] + refs[0][...].astype(jnp.float32)).astype(jnp.bfloat16)
    if shift > 0:
        out_ref[:shift, :] = total[:shift].astype(jnp.bfloat16)
    if to < size:
        out_ref[to:, :] = total[to:].astype(jnp.bfloat16)


def add(own, other, at, size, total=None, shift=0):
    ins = [own, other] + ([] if total is None else [total])
    return kernel(functools.partial(add_body, at, shift), shaped(size, own.shape[1]), ins)


def finish_body(merged_ref, *refs):
    out_ref = refs[-1]
    at = 0
    for index in range(0, len(refs) - 1, 4):
        ins = refs[index : index + 4]
        to = at + ins[0].shape[0]
        total = sum(ref[...].astype(jnp.float32) for ref in ins)
        out_ref[at:to, :] = (merged_ref[at:to, :] + total).astype(jnp.bfloat16)
        at = to


def dense(
    merger_input,
    merger_weight,
    merger_bias,
    norm_gain,
    gate_weight,
    up_weight,
    down_weight,
    expert_ids,
    combine_ints,
):
    n = lax.axis_size(DP)
    chips = n // 2
    far = chips // 2
    rows = merger_input.shape[0]
    depth, width = merger_weight.shape
    half = depth // 2
    cut = rows // 2

    swap = functools.partial(lax.ppermute, axis_name=DP, perm=swap_pairs(n))
    cross = functools.partial(lax.ppermute, axis_name=GROUPS, perm=swap_pairs(2))
    rings = [functools.partial(lax.ppermute, axis_name=DP, perm=ring_pairs(chips, by)) for by in (1, -1)]

    def hop(way, array):
        return rings[way](array)

    first = lax.axis_index(GROUPS).astype(jnp.uint32) * half
    weight = lax.dynamic_slice(merger_weight, (first, jnp.uint32(0)), (half, width))
    block = jax.ShapeDtypeStruct((2, chips, rows, half), jnp.bfloat16)
    mine, given = kernel(functools.partial(gelu_body, chips), [block, block], [merger_input])
    given = swap(given)
    crossed = jnp.stack([mine[1], given[1]])
    crossed = cross(crossed)

    lanes = -(-2 * n // LANES) * LANES
    tags = kernel(functools.partial(tag_body, n), shaped(cut, lanes), [expert_ids.T, combine_ints.T])

    mid = (half + 15) // 16 * 8
    share = width // PARTS
    streams = []
    for part in range(PARTS):
        left = right = weight[:, part * share : (part + 1) * share]
        offsets, pieces = [0], [left]
        for step in range(1, far):
            left, right = hop(0, left), hop(1, right)
            offsets += [chips - step, step]
            pieces += [left, right]
        top, bottom = hop(0, left[:mid]), hop(1, right[mid:])
        size = 4 * rows * share
        total = kernel(
            functools.partial(bulk_body, chips, offsets),
            shaped(4 * rows, share, jnp.float32),
            [mine, given, crossed, *pieces],
            flops=2 * size * half * chips,
            moved=4 * size,
        )
        own, own_other, theirs, theirs_other = kernel(
            functools.partial(last_body, chips),
            [shaped(rows, share, jnp.float32)] * 4,
            [mine, given, crossed, total, top, bottom],
            flops=2 * size * half,
            moved=8 * size,
        )
        theirs_other = swap(theirs_other)
        theirs = kernel(plus_body, shaped(rows, share), [theirs, theirs_other])
        theirs = cross(theirs)
        streams += [own, swap(own_other), theirs]
    merged, *block = kernel(
        functools.partial(norm_body, PARTS),
        [shaped(rows, width, jnp.float32), shaped(cut, width + lanes), shaped(cut, width)],
        [*streams, merger_bias[None], norm_gain[None], tags],
    )

    experts = [w[0] for w in (gate_weight, up_weight, down_weight)]
    arrived = [[(own,) for own in block]]
    sides = [(own, own) for own in block]
    for _ in range(1, far):
        sides = [tuple(hop(way, side[way]) for way in (0, 1)) for side in sides]
        arrived.append(sides)
    short = cut // 2
    arrived.append([(hop(0, side[0][:short]), hop(1, side[1][short:])) for side in sides])

    outs = []
    for step, pair in enumerate(arrived):
        tagged = []
        outs.append([])
        for which, ins in enumerate(pair):
            ins = [*ins, *(swap(x) for x in ins)]
            own, other = serve(which, ins, tagged, experts)
            tagged = ins
            outs[step].append((own, swap(other)))

    def home(way, which):
        total = add(*outs[far][which], way * short, short)
        total = hop(way, total)
        for step in reversed(range(1, far)):
            total = add(*outs[step][which], (1 - way) * cut, cut, total, way * short if step == far - 1 else 0)
            total = hop(way, total)
        return total

    sums = [(*outs[0][which], home(0, which), home(1, which)) for which in (0, 1)]
    return kernel(finish_body, shaped(rows, width), [merged, *sums[0], *sums[1]])


def shards(*arrays):
    gate_weight, expert_ids = arrays[4], arrays[7]
    n = lax.axis_size(DP)
    rows, choose = expert_ids.shape
    capacity = (3 * rows * choose + 2 * n - 1) // (2 * n)
    if lax.axis_size(GROUPS) == 2 and gate_weight.shape[0] == 1 and n % 4 == 0 and n >= 16 and 2 * capacity >= rows:
        return dense(*arrays)
    return routed(*arrays)


def solution(mesh):
    placed = (
        P(("groups", "dp"), None),
        P("dp", None),
        P(),
        P(),
        P("dp", None, None),
        P("dp", None, None),
        P("dp", None, None),
        P(("groups", "dp"), None),
        P(("groups", "dp"), None),
    )
    return jax.shard_map(
        shards, mesh=mesh, in_specs=placed, out_specs=P(("groups", "dp"), None), check_vma=False
    )
```

```python
import functools
import math

import jax
import jax.numpy as jnp
import numpy as np
from jax import lax
from jax.experimental import pallas as pl
from jax.experimental.pallas import tpu as pltpu
from jax.sharding import PartitionSpec as P


LANES = 128
MIB = 1024 * 1024
PARTS = 2
DP = "dp"
GROUPS = "groups"
VMEM = pl.BlockSpec(memory_space=pltpu.VMEM)


def run_experts(received, gate_weight, up_weight, down_weight, ndevices):
    local = gate_weight.shape[0]
    slots = received.shape[1]
    width = received.shape[2]
    inputs = received.reshape(ndevices, local, slots, width)
    gate = jnp.einsum("jlcd,ldh->jlch", inputs, gate_weight, preferred_element_type=jnp.float32)
    up = jnp.einsum("jlcd,ldh->jlch", inputs, up_weight, preferred_element_type=jnp.float32)
    hidden = (jax.nn.silu(gate) * up).astype(jnp.bfloat16)
    output = jnp.einsum("jlch,lhd->jlcd", hidden, down_weight, preferred_element_type=jnp.float32)
    return output.astype(jnp.bfloat16).reshape(ndevices * local, slots, width)


def routed(
    merger_input,
    merger_weight,
    merger_bias,
    norm_gain,
    gate_weight,
    up_weight,
    down_weight,
    expert_ids,
    combine_ints,
):
    ndevices = lax.axis_size("dp")
    rows = merger_input.shape[0]
    width = merger_weight.shape[1]
    choose = expert_ids.shape[1]
    experts_all = gate_weight.shape[0] * ndevices
    capacity = (3 * rows * choose + 2 * ndevices - 1) // (2 * ndevices)
    act = jax.nn.gelu(merger_input.astype(jnp.float32), approximate=False).astype(jnp.bfloat16)
    merged = jnp.dot(
        act,
        lax.all_gather(merger_weight, "dp", axis=0, tiled=True),
        preferred_element_type=jnp.float32,
    )
    merged = merged + merger_bias
    scale = lax.rsqrt(jnp.mean(merged * merged, axis=1, keepdims=True) + 1e-06)
    normed = (merged * scale * norm_gain).astype(jnp.bfloat16)
    onehot = (
        expert_ids[:, :, None] == jnp.arange(experts_all, dtype=jnp.int32)[None, None, :]
    ).astype(jnp.int32)
    flat_hot = onehot.reshape(rows * choose, experts_all)
    before = jnp.cumsum(flat_hot, axis=0) - flat_hot
    position = jnp.sum(before * flat_hot, axis=1)
    slot_flat = expert_ids.reshape(rows * choose) * capacity + position
    repeated = jnp.repeat(normed, choose, axis=0)
    outgoing = jnp.zeros((experts_all * capacity, width), jnp.bfloat16).at[slot_flat].set(repeated)
    outgoing = outgoing.reshape(experts_all, capacity, width)
    received = lax.all_to_all(outgoing, "dp", split_axis=0, concat_axis=0, tiled=True)
    served = run_experts(received, gate_weight, up_weight, down_weight, ndevices)
    returned = lax.all_to_all(served, "dp", split_axis=0, concat_axis=0, tiled=True)
    returned = returned.reshape(experts_all * capacity, width)
    picked = returned[slot_flat].reshape(rows, choose, width)
    counts = combine_ints.astype(jnp.float32)
    weights = counts / jnp.sum(counts, axis=1, keepdims=True)
    combined = jnp.sum(weights[:, :, None] * picked.astype(jnp.float32), axis=1)
    return (merged + combined).astype(jnp.bfloat16)


def swap_pairs(n):
    return [(i, i ^ 1) for i in range(n)]


def ring_order(chips):
    half = chips // 2
    return [2 * z for z in range(half)] + [2 * z + 1 for z in reversed(range(half))]


def ring_pairs(chips, by):
    order = ring_order(chips)
    pairs = []
    for spot, chip in enumerate(order):
        target = order[(spot + by) % chips]
        pairs += [(2 * chip, 2 * target), (2 * chip + 1, 2 * target + 1)]
    return pairs


def chip_at(chips, offset):
    chip = lax.axis_index(DP) // 2
    spot = jnp.where(chip % 2 == 0, chip // 2, chips - 1 - chip // 2)
    spot = lax.rem(spot + offset, chips)
    return jnp.where(spot < chips // 2, 2 * spot, 2 * (chips - 1 - spot) + 1)


def tile_of(extent, most):
    return max(t for t in range(LANES, most + 1, LANES) if extent % t == 0)


def kernel(body, outs, ins, scratch=(), limit=12 * MIB, flops=0, moved=0):
    return pl.pallas_call(
        body,
        out_shape=outs,
        in_specs=[VMEM] * len(ins),
        out_specs=jax.tree.map(lambda _: VMEM, outs),
        scratch_shapes=list(scratch),
        compiler_params=pltpu.CompilerParams(vmem_limit_bytes=limit),
        cost_estimate=pl.CostEstimate(flops=flops, bytes_accessed=moved, transcendentals=0),
    )(*ins)


def shaped(rows, width, dtype=jnp.bfloat16):
    return jax.ShapeDtypeStruct((rows, width), dtype)


def serve_body(blocks, which, experts, *refs):
    ins, tagged = refs[:blocks], refs[: blocks * (which + 1)][-blocks:]
    gate_ref, up_ref, down_ref, own_ref, other_ref, x_ref, h_ref = refs[blocks * (which + 1) :]
    width, wide = gate_ref.shape
    start = 0
    share = []
    for ref, tag in zip(ins, tagged):
        size = ref.shape[0]
        x_ref[start : start + size, :] = ref[:, :width]
        tags = tag[:, width:].astype(jnp.float32)
        lane = lax.broadcasted_iota(jnp.int32, tags.shape, 1) - which * experts
        chosen = jnp.sum(jnp.where(lane == lax.axis_index(DP), tags, 0.0), axis=1, keepdims=True)
        whole = jnp.sum(jnp.where((lane >= 0) & (lane < experts), tags, 0.0), axis=1, keepdims=True)
        share.append(chosen / whole)
        start += size
    share = jnp.concatenate(share, axis=0)
    tile = tile_of(wide, 384)
    for at in range(0, wide, tile):
        x = x_ref[...]
        gate = jnp.dot(x, gate_ref[:, at : at + tile], preferred_element_type=jnp.float32)
        up = jnp.dot(x, up_ref[:, at : at + tile], preferred_element_type=jnp.float32)
        h_ref[:, at : at + tile] = (gate * lax.logistic(gate) * up * share).astype(jnp.bfloat16)
    half = start // 2
    tile = tile_of(width, 512)
    for at in range(0, width, tile):
        out = jnp.dot(h_ref[...], down_ref[:, at : at + tile], preferred_element_type=jnp.float32)
        own_ref[:, at : at + tile] = out[:half].astype(jnp.bfloat16)
        other_ref[:, at : at + tile] = out[half:].astype(jnp.bfloat16)


def serve(which, ins, tagged, weights):
    rows = sum(x.shape[0] for x in ins)
    width, wide = weights[0].shape
    return kernel(
        functools.partial(serve_body, len(ins), which, lax.axis_size(DP)),
        [shaped(rows // 2, width)] * 2,
        [*ins, *tagged, *weights],
        [pltpu.VMEM((rows, width), jnp.bfloat16), pltpu.VMEM((rows, wide), jnp.bfloat16)],
        24 * MIB,
        6 * rows * width * wide,
        6 * width * wide,
    )


def tag_body(experts, ids_ref, counts_ref, out_ref):
    cut, lanes = out_ref.shape
    lane = lax.broadcasted_iota(jnp.int32, (lanes, ids_ref.shape[1]), 0)
    total = jnp.zeros(lane.shape, jnp.float32)
    for k in range(ids_ref.shape[0]):
        counts = counts_ref[k : k + 1, :].astype(jnp.float32)
        total += jnp.where(lane % experts == ids_ref[k : k + 1, :], counts, 0.0)
    total = total.T
    lane = lax.broadcasted_iota(jnp.int32, (cut, lanes), 1)
    total = jnp.where(lane < experts, total[:cut], jnp.where(lane < 2 * experts, total[cut:], 0.0))
    out_ref[...] = total.astype(jnp.bfloat16)


def gelu_body(chips, in_ref, mine_ref, given_ref):
    half = mine_ref.shape[3]
    first_core = lax.axis_index(DP) % 2 == 0
    first_group = lax.axis_index(GROUPS) == 0
    for chip in range(chips):
        x = in_ref[:, chip * 4 * half : (chip + 1) * 4 * half].astype(jnp.float32)
        act = (0.5 * x * (1.0 + lax.erf(x * np.float32(math.sqrt(0.5))))).astype(jnp.bfloat16)
        cuts = [act[:, at * half : (at + 1) * half] for at in range(4)]
        for ref, near, away in ((mine_ref, 0, 2), (given_ref, 2, 0)):
            low = jnp.where(first_core, cuts[near], cuts[away])
            high = jnp.where(first_core, cuts[near + 1], cuts[away + 1])
            ref[0, chip] = jnp.where(first_group, low, high)
            ref[1, chip] = jnp.where(first_group, high, low)


def rows_of(refs, chip):
    mine_ref, given_ref, theirs_ref = refs
    return jnp.concatenate([mine_ref[0, chip], given_ref[0, chip], theirs_ref[0, chip], theirs_ref[1, chip]], axis=0)


def bulk_body(chips, offsets, *refs):
    pieces, out_ref = refs[3:-1], refs[-1]
    width = out_ref.shape[1]
    tile = tile_of(width, 512)
    for at in range(0, width, tile):
        total = None
        for offset, piece in zip(offsets, pieces):
            act = rows_of(refs[:3], chip_at(chips, offset))
            part = jnp.dot(act, piece[:, at : at + tile], preferred_element_type=jnp.float32)
            total = part if total is None else total + part
        out_ref[:, at : at + tile] = total


def last_body(chips, mine_ref, given_ref, theirs_ref, total_ref, top_ref, bottom_ref, *outs):
    width = total_ref.shape[1]
    mid = top_ref.shape[0]
    rows = outs[0].shape[0]
    tile = tile_of(width, 512)
    act = rows_of((mine_ref, given_ref, theirs_ref), chip_at(chips, chips // 2))
    for at in range(0, width, tile):
        to = at + tile
        total = total_ref[:, at:to]
        total += jnp.dot(act[:, :mid], top_ref[:, at:to], preferred_element_type=jnp.float32)
        total += jnp.dot(act[:, mid:], bottom_ref[:, at:to], preferred_element_type=jnp.float32)
        for index, out in enumerate(outs):
            out[:, at:to] = total[index * rows : (index + 1) * rows]


def norm_body(parts, *refs):
    bias_ref, gain_ref, tags_ref, merged_ref, low_ref, high_ref = refs[3 * parts :]
    width = merged_ref.shape[1]
    cut = low_ref.shape[0]
    low_ref[:, width:] = tags_ref[...]
    at = 0
    square = 0.0
    for index in range(parts):
        own_ref, other_ref, cross_ref = refs[3 * index : 3 * index + 3]
        to = at + own_ref.shape[1]
        merged = own_ref[...] + other_ref[...] + bias_ref[:, at:to] + cross_ref[...].astype(jnp.float32)
        merged_ref[:, at:to] = merged
        square += jnp.sum(merged * merged, axis=1, keepdims=True)
        at = to
    scale = lax.rsqrt(square / width + 1e-06)
    low_ref[:, :width] = (merged_ref[:cut, :] * scale[:cut] * gain_ref[...]).astype(jnp.bfloat16)
    high_ref[...] = (merged_ref[cut:, :] * scale[cut:] * gain_ref[...]).astype(jnp.bfloat16)


def plus_body(*refs):
    refs[-1][...] = (refs[0][...] + refs[1][...]).astype(refs[-1].dtype)


def add_body(at, shift, own_ref, other_ref, *refs):
    out_ref = refs[-1]
    size = out_ref.shape[0]
    total = own_ref[at : at + size, :].astype(jnp.float32) + other_ref[at : at + size, :].astype(jnp.float32)
    if len(refs) == 1:
        out_ref[...] = total.astype(jnp.bfloat16)
        return
    to = shift + refs[0].shape[0]
    out_ref[shift:to, :] = (total[shift:to] + refs[0][...].astype(jnp.float32)).astype(jnp.bfloat16)
    if shift > 0:
        out_ref[:shift, :] = total[:shift].astype(jnp.bfloat16)
    if to < size:
        out_ref[to:, :] = total[to:].astype(jnp.bfloat16)


def add(own, other, at, size, total=None, shift=0):
    ins = [own, other] + ([] if total is None else [total])
    return kernel(functools.partial(add_body, at, shift), shaped(size, own.shape[1]), ins)


def finish_body(merged_ref, *refs):
    out_ref = refs[-1]
    at = 0
    for index in range(0, len(refs) - 1, 4):
        ins = refs[index : index + 4]
        to = at + ins[0].shape[0]
        total = sum(ref[...].astype(jnp.float32) for ref in ins)
        out_ref[at:to, :] = (merged_ref[at:to, :] + total).astype(jnp.bfloat16)
        at = to


def dense(
    merger_input,
    merger_weight,
    merger_bias,
    norm_gain,
    gate_weight,
    up_weight,
    down_weight,
    expert_ids,
    combine_ints,
):
    n = lax.axis_size(DP)
    chips = n // 2
    far = chips // 2
    rows = merger_input.shape[0]
    depth, width = merger_weight.shape
    half = depth // 2
    cut = rows // 2

    swap = functools.partial(lax.ppermute, axis_name=DP, perm=swap_pairs(n))
    cross = functools.partial(lax.ppermute, axis_name=GROUPS, perm=swap_pairs(2))
    rings = [functools.partial(lax.ppermute, axis_name=DP, perm=ring_pairs(chips, by)) for by in (1, -1)]

    def hop(way, array):
        return rings[way](array)

    first = lax.axis_index(GROUPS).astype(jnp.uint32) * half
    weight = lax.dynamic_slice(merger_weight, (first, jnp.uint32(0)), (half, width))
    block = jax.ShapeDtypeStruct((2, chips, rows, half), jnp.bfloat16)
    mine, given = kernel(functools.partial(gelu_body, chips), [block, block], [merger_input])
    given = swap(given)
    crossed = jnp.stack([mine[1], given[1]])
    crossed = cross(crossed)

    lanes = -(-2 * n // LANES) * LANES
    tags = kernel(functools.partial(tag_body, n), shaped(cut, lanes), [expert_ids.T, combine_ints.T])

    mid = (half + 15) // 16 * 8
    share = width // PARTS
    streams = []
    for part in range(PARTS):
        left = right = weight[:, part * share : (part + 1) * share]
        offsets, pieces = [0], [left]
        for step in range(1, far):
            left, right = hop(0, left), hop(1, right)
            offsets += [chips - step, step]
            pieces += [left, right]
        top, bottom = hop(0, left[:mid]), hop(1, right[mid:])
        size = 4 * rows * share
        total = kernel(
            functools.partial(bulk_body, chips, offsets),
            shaped(4 * rows, share, jnp.float32),
            [mine, given, crossed, *pieces],
            flops=2 * size * half * chips,
            moved=4 * size,
        )
        own, own_other, theirs, theirs_other = kernel(
            functools.partial(last_body, chips),
            [shaped(rows, share, jnp.float32)] * 4,
            [mine, given, crossed, total, top, bottom],
            flops=2 * size * half,
            moved=8 * size,
        )
        theirs_other = swap(theirs_other)
        theirs = kernel(plus_body, shaped(rows, share), [theirs, theirs_other])
        theirs = cross(theirs)
        streams += [own, swap(own_other), theirs]
    merged, *block = kernel(
        functools.partial(norm_body, PARTS),
        [shaped(rows, width, jnp.float32), shaped(cut, width + lanes), shaped(cut, width)],
        [*streams, merger_bias[None], norm_gain[None], tags],
    )

    experts = [w[0] for w in (gate_weight, up_weight, down_weight)]
    arrived = [[(own,) for own in block]]
    sides = [(own, own) for own in block]
    for _ in range(1, far):
        sides = [tuple(hop(way, side[way]) for way in (0, 1)) for side in sides]
        arrived.append(sides)
    short = cut // 2
    arrived.append([(hop(0, side[0][:short]), hop(1, side[1][short:])) for side in sides])

    outs = []
    for step, pair in enumerate(arrived):
        tagged = []
        outs.append([])
        for which, ins in enumerate(pair):
            ins = [*ins, *(swap(x) for x in ins)]
            own, other = serve(which, ins, tagged, experts)
            tagged = ins
            outs[step].append((own, swap(other)))

    def home(way, which):
        total = add(*outs[far][which], way * short, short)
        total = hop(way, total)
        for step in reversed(range(1, far)):
            total = add(*outs[step][which], (1 - way) * cut, cut, total, way * short if step == far - 1 else 0)
            total = hop(way, total)
        return total

    sums = [(*outs[0][which], home(0, which), home(1, which)) for which in (0, 1)]
    return kernel(finish_body, shaped(rows, width), [merged, *sums[0], *sums[1]])


def shards(*arrays):
    gate_weight, expert_ids = arrays[4], arrays[7]
    n = lax.axis_size(DP)
    rows, choose = expert_ids.shape
    capacity = (3 * rows * choose + 2 * n - 1) // (2 * n)
    if lax.axis_size(GROUPS) == 2 and gate_weight.shape[0] == 1 and n % 4 == 0 and n >= 16 and 2 * capacity >= rows:
        return dense(*arrays)
    return routed(*arrays)


def solution(mesh):
    placed = (
        P(("groups", "dp"), None),
        P("dp", None),
        P(),
        P(),
        P("dp", None, None),
        P("dp", None, None),
        P("dp", None, None),
        P(("groups", "dp"), None),
        P(("groups", "dp"), None),
    )
    return jax.shard_map(
        shards, mesh=mesh, in_specs=placed, out_specs=P(("groups", "dp"), None), check_vma=False
    )
```

```python
import functools
import math

import jax
import jax.numpy as jnp
import numpy as np
from jax import lax
from jax.experimental import pallas as pl
from jax.experimental.pallas import tpu as pltpu
from jax.sharding import PartitionSpec as P


LANES = 128
MIB = 1024 * 1024
PARTS = 2
DP = "dp"
GROUPS = "groups"
VMEM = pl.BlockSpec(memory_space=pltpu.VMEM)


def run_experts(received, gate_weight, up_weight, down_weight, ndevices):
    local = gate_weight.shape[0]
    slots = received.shape[1]
    width = received.shape[2]
    inputs = received.reshape(ndevices, local, slots, width)
    gate = jnp.einsum("jlcd,ldh->jlch", inputs, gate_weight, preferred_element_type=jnp.float32)
    up = jnp.einsum("jlcd,ldh->jlch", inputs, up_weight, preferred_element_type=jnp.float32)
    hidden = (jax.nn.silu(gate) * up).astype(jnp.bfloat16)
    output = jnp.einsum("jlch,lhd->jlcd", hidden, down_weight, preferred_element_type=jnp.float32)
    return output.astype(jnp.bfloat16).reshape(ndevices * local, slots, width)


def routed(
    merger_input,
    merger_weight,
    merger_bias,
    norm_gain,
    gate_weight,
    up_weight,
    down_weight,
    expert_ids,
    combine_ints,
):
    ndevices = lax.axis_size("dp")
    rows = merger_input.shape[0]
    width = merger_weight.shape[1]
    choose = expert_ids.shape[1]
    experts_all = gate_weight.shape[0] * ndevices
    capacity = (3 * rows * choose + 2 * ndevices - 1) // (2 * ndevices)
    act = jax.nn.gelu(merger_input.astype(jnp.float32), approximate=False).astype(jnp.bfloat16)
    merged = jnp.dot(
        act,
        lax.all_gather(merger_weight, "dp", axis=0, tiled=True),
        preferred_element_type=jnp.float32,
    )
    merged = merged + merger_bias
    scale = lax.rsqrt(jnp.mean(merged * merged, axis=1, keepdims=True) + 1e-06)
    normed = (merged * scale * norm_gain).astype(jnp.bfloat16)
    onehot = (
        expert_ids[:, :, None] == jnp.arange(experts_all, dtype=jnp.int32)[None, None, :]
    ).astype(jnp.int32)
    flat_hot = onehot.reshape(rows * choose, experts_all)
    before = jnp.cumsum(flat_hot, axis=0) - flat_hot
    position = jnp.sum(before * flat_hot, axis=1)
    slot_flat = expert_ids.reshape(rows * choose) * capacity + position
    repeated = jnp.repeat(normed, choose, axis=0)
    outgoing = jnp.zeros((experts_all * capacity, width), jnp.bfloat16).at[slot_flat].set(repeated)
    outgoing = outgoing.reshape(experts_all, capacity, width)
    received = lax.all_to_all(outgoing, "dp", split_axis=0, concat_axis=0, tiled=True)
    served = run_experts(received, gate_weight, up_weight, down_weight, ndevices)
    returned = lax.all_to_all(served, "dp", split_axis=0, concat_axis=0, tiled=True)
    returned = returned.reshape(experts_all * capacity, width)
    picked = returned[slot_flat].reshape(rows, choose, width)
    counts = combine_ints.astype(jnp.float32)
    weights = counts / jnp.sum(counts, axis=1, keepdims=True)
    combined = jnp.sum(weights[:, :, None] * picked.astype(jnp.float32), axis=1)
    return (merged + combined).astype(jnp.bfloat16)


def swap_pairs(n):
    return [(i, i ^ 1) for i in range(n)]


def ring_order(chips):
    half = chips // 2
    return [2 * z for z in range(half)] + [2 * z + 1 for z in reversed(range(half))]


def ring_pairs(chips, by):
    order = ring_order(chips)
    pairs = []
    for spot, chip in enumerate(order):
        target = order[(spot + by) % chips]
        pairs += [(2 * chip, 2 * target), (2 * chip + 1, 2 * target + 1)]
    return pairs


def chip_at(chips, offset):
    chip = lax.axis_index(DP) // 2
    spot = jnp.where(chip % 2 == 0, chip // 2, chips - 1 - chip // 2)
    spot = lax.rem(spot + offset, chips)
    return jnp.where(spot < chips // 2, 2 * spot, 2 * (chips - 1 - spot) + 1)


def tile_of(extent, most):
    return max(t for t in range(LANES, most + 1, LANES) if extent % t == 0)


def kernel(body, outs, ins, scratch=(), limit=12 * MIB, flops=0, moved=0):
    return pl.pallas_call(
        body,
        out_shape=outs,
        in_specs=[VMEM] * len(ins),
        out_specs=jax.tree.map(lambda _: VMEM, outs),
        scratch_shapes=list(scratch),
        compiler_params=pltpu.CompilerParams(vmem_limit_bytes=limit),
        cost_estimate=pl.CostEstimate(flops=flops, bytes_accessed=moved, transcendentals=0),
    )(*ins)


def shaped(rows, width, dtype=jnp.bfloat16):
    return jax.ShapeDtypeStruct((rows, width), dtype)


def serve_body(blocks, which, experts, *refs):
    ins, tagged = refs[:blocks], refs[: blocks * (which + 1)][-blocks:]
    gate_ref, up_ref, down_ref, own_ref, other_ref, x_ref, h_ref = refs[blocks * (which + 1) :]
    width, wide = gate_ref.shape
    start = 0
    share = []
    for ref, tag in zip(ins, tagged):
        size = ref.shape[0]
        x_ref[start : start + size, :] = ref[:, :width]
        tags = tag[:, width:].astype(jnp.float32)
        lane = lax.broadcasted_iota(jnp.int32, tags.shape, 1) - which * experts
        chosen = jnp.sum(jnp.where(lane == lax.axis_index(DP), tags, 0.0), axis=1, keepdims=True)
        whole = jnp.sum(jnp.where((lane >= 0) & (lane < experts), tags, 0.0), axis=1, keepdims=True)
        share.append(chosen / whole)
        start += size
    share = jnp.concatenate(share, axis=0)
    tile = tile_of(wide, 256)
    for at in range(0, wide, tile):
        x = x_ref[...]
        gate = jnp.dot(x, gate_ref[:, at : at + tile], preferred_element_type=jnp.float32)
        up = jnp.dot(x, up_ref[:, at : at + tile], preferred_element_type=jnp.float32)
        h_ref[:, at : at + tile] = (gate * (1.0 / (1.0 + jnp.exp(-gate))) * up * share).astype(jnp.bfloat16)
    half = start // 2
    tile = tile_of(width, 256)
    for at in range(0, width, tile):
        out = jnp.dot(h_ref[...], down_ref[:, at : at + tile], preferred_element_type=jnp.float32)
        own_ref[:, at : at + tile] = out[:half].astype(jnp.bfloat16)
        other_ref[:, at : at + tile] = out[half:].astype(jnp.bfloat16)


def serve(which, ins, tagged, weights):
    rows = sum(x.shape[0] for x in ins)
    width, wide = weights[0].shape
    return kernel(
        functools.partial(serve_body, len(ins), which, lax.axis_size(DP)),
        [shaped(rows // 2, width)] * 2,
        [*ins, *tagged, *weights],
        [pltpu.VMEM((rows, width), jnp.bfloat16), pltpu.VMEM((rows, wide), jnp.bfloat16)],
        24 * MIB,
        6 * rows * width * wide,
        6 * width * wide,
    )


def tag_body(experts, ids_ref, counts_ref, out_ref):
    cut, lanes = out_ref.shape
    lane = lax.broadcasted_iota(jnp.int32, (lanes, ids_ref.shape[1]), 0)
    total = jnp.zeros(lane.shape, jnp.float32)
    for k in range(ids_ref.shape[0]):
        counts = counts_ref[k : k + 1, :].astype(jnp.float32)
        total += jnp.where(lane % experts == ids_ref[k : k + 1, :], counts, 0.0)
    total = total.T
    lane = lax.broadcasted_iota(jnp.int32, (cut, lanes), 1)
    total = jnp.where(lane < experts, total[:cut], jnp.where(lane < 2 * experts, total[cut:], 0.0))
    out_ref[...] = total.astype(jnp.bfloat16)


def gelu_body(chips, in_ref, mine_ref, given_ref):
    half = mine_ref.shape[3]
    first_core = lax.axis_index(DP) % 2 == 0
    first_group = lax.axis_index(GROUPS) == 0
    for chip in range(chips):
        x = in_ref[:, chip * 4 * half : (chip + 1) * 4 * half].astype(jnp.float32)
        act = (0.5 * x * (1.0 + lax.erf(x * np.float32(math.sqrt(0.5))))).astype(jnp.bfloat16)
        cuts = [act[:, at * half : (at + 1) * half] for at in range(4)]
        for ref, near, away in ((mine_ref, 0, 2), (given_ref, 2, 0)):
            low = jnp.where(first_core, cuts[near], cuts[away])
            high = jnp.where(first_core, cuts[near + 1], cuts[away + 1])
            ref[0, chip] = jnp.where(first_group, low, high)
            ref[1, chip] = jnp.where(first_group, high, low)


def rows_of(refs, chip):
    mine_ref, given_ref, theirs_ref = refs
    return jnp.concatenate([mine_ref[0, chip], given_ref[0, chip], theirs_ref[0, chip], theirs_ref[1, chip]], axis=0)


def bulk_body(chips, offsets, *refs):
    pieces, out_ref = refs[3:-1], refs[-1]
    width = out_ref.shape[1]
    tile = tile_of(width, 256)
    for at in range(0, width, tile):
        total = None
        for offset, piece in zip(offsets, pieces):
            act = rows_of(refs[:3], chip_at(chips, offset))
            part = jnp.dot(act, piece[:, at : at + tile], preferred_element_type=jnp.float32)
            total = part if total is None else total + part
        out_ref[:, at : at + tile] = total


def last_body(chips, mine_ref, given_ref, theirs_ref, total_ref, top_ref, bottom_ref, *outs):
    width = total_ref.shape[1]
    mid = top_ref.shape[0]
    rows = outs[0].shape[0]
    tile = tile_of(width, 256)
    act = rows_of((mine_ref, given_ref, theirs_ref), chip_at(chips, chips // 2))
    for at in range(0, width, tile):
        to = at + tile
        total = total_ref[:, at:to]
        total += jnp.dot(act[:, :mid], top_ref[:, at:to], preferred_element_type=jnp.float32)
        total += jnp.dot(act[:, mid:], bottom_ref[:, at:to], preferred_element_type=jnp.float32)
        for index, out in enumerate(outs):
            out[:, at:to] = total[index * rows : (index + 1) * rows]


def norm_body(parts, *refs):
    bias_ref, gain_ref, tags_ref, merged_ref, low_ref, high_ref = refs[3 * parts :]
    width = merged_ref.shape[1]
    cut = low_ref.shape[0]
    low_ref[:, width:] = tags_ref[...]
    at = 0
    square = 0.0
    for index in range(parts):
        own_ref, other_ref, cross_ref = refs[3 * index : 3 * index + 3]
        to = at + own_ref.shape[1]
        merged = own_ref[...] + other_ref[...] + bias_ref[:, at:to] + cross_ref[...].astype(jnp.float32)
        merged_ref[:, at:to] = merged
        square += jnp.sum(merged * merged, axis=1, keepdims=True)
        at = to
    scale = lax.rsqrt(square / width + 1e-06)
    low_ref[:, :width] = (merged_ref[:cut, :] * scale[:cut] * gain_ref[...]).astype(jnp.bfloat16)
    high_ref[...] = (merged_ref[cut:, :] * scale[cut:] * gain_ref[...]).astype(jnp.bfloat16)


def plus_body(*refs):
    refs[-1][...] = (refs[0][...] + refs[1][...]).astype(refs[-1].dtype)


def add_body(at, shift, own_ref, other_ref, *refs):
    out_ref = refs[-1]
    size = out_ref.shape[0]
    total = own_ref[at : at + size, :].astype(jnp.float32) + other_ref[at : at + size, :].astype(jnp.float32)
    if len(refs) == 1:
        out_ref[...] = total.astype(jnp.bfloat16)
        return
    to = shift + refs[0].shape[0]
    out_ref[shift:to, :] = (total[shift:to] + refs[0][...].astype(jnp.float32)).astype(jnp.bfloat16)
    if shift > 0:
        out_ref[:shift, :] = total[:shift].astype(jnp.bfloat16)
    if to < size:
        out_ref[to:, :] = total[to:].astype(jnp.bfloat16)


def add(own, other, at, size, total=None, shift=0):
    ins = [own, other] + ([] if total is None else [total])
    return kernel(functools.partial(add_body, at, shift), shaped(size, own.shape[1]), ins)


def finish_body(merged_ref, *refs):
    out_ref = refs[-1]
    at = 0
    for index in range(0, len(refs) - 1, 4):
        ins = refs[index : index + 4]
        to = at + ins[0].shape[0]
        total = sum(ref[...].astype(jnp.float32) for ref in ins)
        out_ref[at:to, :] = (merged_ref[at:to, :] + total).astype(jnp.bfloat16)
        at = to


def dense(
    merger_input,
    merger_weight,
    merger_bias,
    norm_gain,
    gate_weight,
    up_weight,
    down_weight,
    expert_ids,
    combine_ints,
):
    n = lax.axis_size(DP)
    chips = n // 2
    far = chips // 2
    rows = merger_input.shape[0]
    depth, width = merger_weight.shape
    half = depth // 2
    cut = rows // 2

    swap = functools.partial(lax.ppermute, axis_name=DP, perm=swap_pairs(n))
    cross = functools.partial(lax.ppermute, axis_name=GROUPS, perm=swap_pairs(2))
    rings = [functools.partial(lax.ppermute, axis_name=DP, perm=ring_pairs(chips, by)) for by in (1, -1)]

    def hop(way, array):
        return rings[way](array)

    first = lax.axis_index(GROUPS).astype(jnp.uint32) * half
    weight = lax.dynamic_slice(merger_weight, (first, jnp.uint32(0)), (half, width))
    block = jax.ShapeDtypeStruct((2, chips, rows, half), jnp.bfloat16)
    mine, given = kernel(functools.partial(gelu_body, chips), [block, block], [merger_input])
    given = swap(given)
    crossed = jnp.stack([mine[1], given[1]])
    crossed = cross(crossed)

    lanes = -(-2 * n // LANES) * LANES
    tags = kernel(functools.partial(tag_body, n), shaped(cut, lanes), [expert_ids.T, combine_ints.T])

    mid = (half + 15) // 16 * 8
    share = width // PARTS
    streams = []
    for part in range(PARTS):
        left = right = weight[:, part * share : (part + 1) * share]
        offsets, pieces = [0], [left]
        for step in range(1, far):
            left, right = hop(0, left), hop(1, right)
            offsets += [chips - step, step]
            pieces += [left, right]
        top, bottom = hop(0, left[:mid]), hop(1, right[mid:])
        size = 4 * rows * share
        total = kernel(
            functools.partial(bulk_body, chips, offsets),
            shaped(4 * rows, share, jnp.float32),
            [mine, given, crossed, *pieces],
            flops=2 * size * half * chips,
            moved=4 * size,
        )
        own, own_other, theirs, theirs_other = kernel(
            functools.partial(last_body, chips),
            [shaped(rows, share, jnp.float32)] * 4,
            [mine, given, crossed, total, top, bottom],
            flops=2 * size * half,
            moved=8 * size,
        )
        theirs_other = swap(theirs_other)
        theirs = kernel(plus_body, shaped(rows, share), [theirs, theirs_other])
        theirs = cross(theirs)
        streams += [own, swap(own_other), theirs]
    merged, *block = kernel(
        functools.partial(norm_body, PARTS),
        [shaped(rows, width, jnp.float32), shaped(cut, width + lanes), shaped(cut, width)],
        [*streams, merger_bias[None], norm_gain[None], tags],
    )

    experts = [w[0] for w in (gate_weight, up_weight, down_weight)]
    arrived = [[(own,) for own in block]]
    sides = [(own, own) for own in block]
    for _ in range(1, far):
        sides = [tuple(hop(way, side[way]) for way in (0, 1)) for side in sides]
        arrived.append(sides)
    short = cut // 2
    arrived.append([(hop(0, side[0][:short]), hop(1, side[1][short:])) for side in sides])

    outs = []
    for step, pair in enumerate(arrived):
        tagged = []
        outs.append([])
        for which, ins in enumerate(pair):
            ins = [*ins, *(swap(x) for x in ins)]
            own, other = serve(which, ins, tagged, experts)
            tagged = ins
            outs[step].append((own, swap(other)))

    def home(way, which):
        total = add(*outs[far][which], way * short, short)
        total = hop(way, total)
        for step in reversed(range(1, far)):
            total = add(*outs[step][which], (1 - way) * cut, cut, total, way * short if step == far - 1 else 0)
            total = hop(way, total)
        return total

    sums = [(*outs[0][which], home(0, which), home(1, which)) for which in (0, 1)]
    return kernel(finish_body, shaped(rows, width), [merged, *sums[0], *sums[1]])


def shards(*arrays):
    gate_weight, expert_ids = arrays[4], arrays[7]
    n = lax.axis_size(DP)
    rows, choose = expert_ids.shape
    capacity = (3 * rows * choose + 2 * n - 1) // (2 * n)
    if lax.axis_size(GROUPS) == 2 and gate_weight.shape[0] == 1 and n % 4 == 0 and n >= 16 and 2 * capacity >= rows:
        return dense(*arrays)
    return routed(*arrays)


def solution(mesh):
    placed = (
        P(("groups", "dp"), None),
        P("dp", None),
        P(),
        P(),
        P("dp", None, None),
        P("dp", None, None),
        P("dp", None, None),
        P(("groups", "dp"), None),
        P(("groups", "dp"), None),
    )
    return jax.shard_map(
        shards, mesh=mesh, in_specs=placed, out_specs=P(("groups", "dp"), None), check_vma=False
    )
```
